256 devices in a mesh: blk: 256 (over z, x, y, core).
Axes of the slice: x: 4, y: 4, z: 8, core: 2. Of those that a mesh axis runs over, the one named last changes fastest.
Arguments:
- features: float32 [65536, 128], P('blk'), may hold values from -6 to 6
- weight_one: float32 [128, 128], replicated, may hold values from -0.5 to 0.5
- weight_two: float32 [128, 128], replicated, may hold values from -0.5 to 0.5
- dense_tiles: bfloat16 [65536, 128, 128], P('blk'), may hold values from -0.0390625 to 0.0390625
- dense_row: int32 [65536], P('blk'), may hold values from 0 to 1
- hub_block: int32 [256], replicated, may hold values from 0 to 1
- sparse_tiles: bfloat16 [28672, 128, 128], P('blk'), may hold values from -0.0390625 to 0.0390625
- sparse_row: int32 [28672], P('blk'), may hold values from 0 to 1
- sparse_src: int32 [28672], P('blk'), may hold values from 0 to 5
- sparse_count: int32 [256], P('blk'), may hold values from 1 to 112, as said below
- fetch_list: int32 [256, 4], P('blk'), may hold values from 0 to 1
Outputs:
- embedded: float32 [65536, 128], P('blk')
The draws below stay inside these ranges and needn't reach their ends.
Inputs may be any that keep to these rules, and one draw needn't show every extreme that they name: `sparse_count`: one device has exactly 112 live slots.
All inputs are finite; a program needn't handle non-finite values.
Results may differ from the reference program's by a relative error of at most 0.0041.
Values may be sent and summed in bfloat16 or wider, within the bound.
No kernel may reach another device: no remote copies, remote signals or barrier semaphores. Data moves between devices by JAX's collectives and lax.ppermute only.
A program may use at most 128 MiB of HBM per device.

```python
import jax
import jax.numpy as jnp
from jax import lax

F = 128
TILE = 128
NB = 2
KS = 112
HOPS = 2
FETCH = 1
NODES = 65536
N_BLK = 256


def draw_sparse_count(key, part):
    first_key, second_key = jax.random.split(jax.random.fold_in(key, 7))
    levels = jax.random.randint(first_key, (N_BLK,), 0, 16)
    counts = jnp.maximum(KS * levels * levels // 225, KS // 16 + 1)
    busiest = jax.random.randint(second_key, (), 0, N_BLK)
    counts = jnp.where(jnp.arange(N_BLK) == busiest, KS, counts)
    return counts.astype(jnp.int32)


def set_ends(values, rng, low, top_value):
    dims = values.shape
    index_at = [jax.random.randint(jax.random.fold_in(rng, axis), (), 0, dims[axis]) for axis in range(len(dims))]
    values = values.at[tuple(index_at)].set(low)
    longest = dims.index(max(dims))
    index_at[longest] = (index_at[longest] + 1) % dims[longest]
    return values.at[tuple(index_at)].set(top_value)


def shard_levels(own_key, shape, cuts, smallest, high):
    def one(position, shards_of):
        draws = jax.random.uniform(jax.random.fold_in(jax.random.fold_in(own_key, 6), position), (shards_of,), jnp.float32, smallest / len(cuts), high / len(cuts))
        return jnp.repeat(jnp.exp(draws), shape[position] // shards_of).reshape((-1,) + (1,) * (len(shape) - position - 1))

    level = one(*cuts[0])
    for cut in cuts[1:]:
        level = level * one(*cut)
    return level


def centred(key, shape, width, limit, cuts=(), kind=jnp.bfloat16):
    entries = width * jax.random.normal(key, shape, jnp.float32)
    if cuts:
        entries = entries * shard_levels(key, shape, cuts, -0.22, 0.18)
    return jnp.clip(entries, -limit, limit).astype(kind)


def setup_inputs(seed: int = 0) -> dict:
    arg_keys = jax.random.split(jax.random.key(seed), 12)
    features = centred(arg_keys[0], (NODES, F), 1.0, 6.0, ((0, 256),), jnp.float32)
    weight_one = centred(arg_keys[1], (F, F), F ** -0.5, 0.5, (), jnp.float32)
    weight_two = centred(arg_keys[2], (F, F), F ** -0.5, 0.5, (), jnp.float32)
    dense_tiles = centred(arg_keys[3], (N_BLK * N_BLK, TILE, TILE), (TILE * (N_BLK // NB + KS // (2 * NB))) ** -0.5, 0.0390625, ((0, 256),))
    dense_row = set_ends(jax.random.randint(arg_keys[4], (N_BLK * N_BLK,), 0, NB), jax.random.fold_in(arg_keys[4], 1), 0, NB - 1).astype(jnp.int32)
    hub_block = set_ends(jax.random.randint(arg_keys[5], (N_BLK,), 0, NB), jax.random.fold_in(arg_keys[5], 1), 0, NB - 1).astype(jnp.int32)
    sparse_tiles = centred(arg_keys[6], (N_BLK * KS, TILE, TILE), (TILE * (N_BLK // NB + KS // (2 * NB))) ** -0.5, 0.0390625, ((0, 256),))
    sparse_row = set_ends(jax.random.randint(arg_keys[7], (N_BLK * KS,), 0, NB), jax.random.fold_in(arg_keys[7], 1), 0, NB - 1).astype(jnp.int32)
    sparse_src = set_ends(jax.random.randint(arg_keys[8], (N_BLK * KS,), 0, NB + 2 * HOPS * FETCH), jax.random.fold_in(arg_keys[8], 1), 0, (NB + 2 * HOPS * FETCH) - 1).astype(jnp.int32)
    sparse_count = draw_sparse_count(jax.random.fold_in(arg_keys[11], 71), 0)
    fetch_list = set_ends(jax.random.randint(arg_keys[10], (N_BLK, 2 * HOPS * FETCH), 0, NB), jax.random.fold_in(arg_keys[10], 1), 0, NB - 1).astype(jnp.int32)
    return {"features": features, "weight_one": weight_one, "weight_two": weight_two, "dense_tiles": dense_tiles, "dense_row": dense_row, "hub_block": hub_block, "sparse_tiles": sparse_tiles, "sparse_row": sparse_row, "sparse_src": sparse_src, "sparse_count": sparse_count, "fetch_list": fetch_list}


def neighbour_offsets():
    return list(range(-HOPS, 0)) + list(range(1, HOPS + 1))


def reference(features, weight_one, weight_two, dense_tiles, dense_row, hub_block, sparse_tiles, sparse_row, sparse_src, sparse_count, fetch_list):
    offsets = neighbour_offsets()
    owner_shift = jnp.array([offsets[entry // FETCH] for entry in range(2 * HOPS * FETCH)], dtype=jnp.int32)
    block_ids = jnp.arange(NB, dtype=jnp.int32)
    slot_ids = jnp.arange(KS, dtype=jnp.int32)
    device_ids = jnp.arange(N_BLK, dtype=jnp.int32)

    def propagate(hidden_rows, weight):
        blocks = hidden_rows.reshape(N_BLK, NB, TILE, F)
        hub_rows = blocks[device_ids, hub_block].astype(jnp.float32)

        def one_device(device):
            dense_start = (device * N_BLK).astype(jnp.int32)
            tile_set = lax.dynamic_slice_in_dim(dense_tiles, dense_start, N_BLK, 0).astype(jnp.float32)
            row_ids = lax.dynamic_slice_in_dim(dense_row, dense_start, N_BLK, 0)
            products = jnp.einsum("sij,sjf->sif", tile_set, hub_rows)
            onehot = (row_ids[:, None] == block_ids[None, :]).astype(jnp.float32)
            summed = jnp.einsum("sn,sif->nif", onehot, products, precision=lax.Precision.HIGHEST)
            owners = ((device + owner_shift) % N_BLK).astype(jnp.int32)
            wanted = lax.dynamic_index_in_dim(fetch_list, device, 0, keepdims=False)
            fetched = blocks[owners, wanted]
            own_blocks = lax.dynamic_index_in_dim(blocks, device, 0, keepdims=False)
            gathered_blocks = jnp.concatenate([own_blocks, fetched], axis=0)
            sparse_start = (device * KS).astype(jnp.int32)
            sparse_set = lax.dynamic_slice_in_dim(sparse_tiles, sparse_start, KS, 0).astype(jnp.float32)
            sparse_rows = lax.dynamic_slice_in_dim(sparse_row, sparse_start, KS, 0)
            sources = lax.dynamic_slice_in_dim(sparse_src, sparse_start, KS, 0)
            inputs = gathered_blocks[sources].astype(jnp.float32)
            sparse_products = jnp.einsum("kij,kjf->kif", sparse_set, inputs)
            live_total = lax.dynamic_index_in_dim(sparse_count, device, 0, keepdims=False)
            live_mask = (slot_ids < live_total).astype(jnp.float32)
            sparse_onehot = (sparse_rows[:, None] == block_ids[None, :]).astype(jnp.float32) * live_mask[:, None]
            summed = summed + jnp.einsum("kn,kif->nif", sparse_onehot, sparse_products, precision=lax.Precision.HIGHEST)
            return summed.reshape(NB * TILE, F)

        summed_all = lax.map(one_device, device_ids)
        projected = jnp.dot(summed_all.reshape(N_BLK * NB * TILE, F), weight, precision=lax.Precision.HIGHEST, preferred_element_type=jnp.float32)
        return jax.nn.relu(projected)

    inputs_first = features.astype(jnp.bfloat16)
    hidden = propagate(inputs_first, weight_one).astype(jnp.bfloat16)
    return propagate(hidden, weight_two)
```

```python
import functools

import jax
import jax.numpy as jnp
from jax import lax
from jax.experimental import pallas as pl
from jax.experimental.pallas import tpu as pltpu
from jax.sharding import PartitionSpec as P

F = 128
TILE = 128
NB = 2
KS = 112
HOPS = 2
FETCH = 1
SOURCES = NB + 2 * HOPS * FETCH


def from_behind(shard, axis, by):
    size = lax.axis_size(axis)
    return lax.ppermute(shard, axis, [(i, (i + by) % size) for i in range(size)])


def neighbour_offsets():
    return list(range(-HOPS, 0)) + list(range(1, HOPS + 1))


def placed_pair(block, row):
    zeros = jnp.zeros_like(block)
    return jnp.concatenate([jnp.where(row == 0, block, zeros), jnp.where(row == 0, zeros, block)], axis=1)


def sparse_kernel(row_ref, src_ref, count_ref, fetch_ref, blocks_ref, *refs):
    fetched_refs, (tiles_ref, out_ref, placed_ref) = refs[: 2 * HOPS], refs[2 * HOPS :]
    zeros = jnp.zeros((TILE, F), jnp.bfloat16)
    for source in range(SOURCES):
        if source < NB:
            block = blocks_ref[source]
        else:
            block = fetched_refs[source - NB][fetch_ref[source - NB]]
        placed_ref[2 * source] = jnp.concatenate([block, zeros], axis=1)
        placed_ref[2 * source + 1] = jnp.concatenate([zeros, block], axis=1)
    placed_ref[2 * SOURCES] = jnp.zeros((TILE, NB * F), jnp.bfloat16)
    out_ref[...] = jnp.zeros_like(out_ref)
    live = count_ref[0]

    def which(slot):
        return jnp.where(slot < live, 2 * src_ref[slot] + row_ref[slot], 2 * SOURCES)

    group = 8

    def step(at, _):
        first = at * group
        left = jnp.concatenate([tiles_ref[first + k] for k in range(group)], axis=1)
        right = jnp.concatenate([placed_ref[which(first + k)] for k in range(group)], axis=0)
        out_ref[...] += jnp.dot(left, right, preferred_element_type=jnp.float32)
        return 0

    lax.fori_loop(0, (live + group - 1) // group, step, 0)


def sparse_sums(row, src, count, wanted, blocks, fetched, tiles):
    smem = pl.BlockSpec(memory_space=pltpu.SMEM)
    vmem = pl.BlockSpec(memory_space=pltpu.VMEM)
    return pl.pallas_call(
        sparse_kernel,
        out_shape=jax.ShapeDtypeStruct((TILE, NB * F), jnp.float32),
        in_specs=[smem] * 4 + [vmem] * (2 + 2 * HOPS),
        out_specs=vmem,
        scratch_shapes=[pltpu.VMEM((2 * SOURCES + 1, TILE, NB * F), jnp.bfloat16)],
        name="sparse_sums",
    )(row, src, count, wanted, blocks, *fetched, tiles)


def dense_kernel(group, row_ref, stripe_ref, tiles_ref, start_ref, weight_ref, out_ref, total):
    at = pl.program_id(0)

    @pl.when(at == 0)
    def _():
        total[...] = start_ref[...]

    first = at * group
    left = jnp.concatenate([tiles_ref[k] for k in range(group)], axis=1)
    right = jnp.concatenate([placed_pair(stripe_ref[k], row_ref[first + k]) for k in range(group)], axis=0)
    total[...] += jnp.dot(left, right, preferred_element_type=jnp.float32)

    @pl.when(at == pl.num_programs(0) - 1)
    def _():
        for block in range(NB):
            projected = jnp.dot(
                total[:, block * F : (block + 1) * F],
                weight_ref[...],
                precision=lax.Precision.HIGHEST,
                preferred_element_type=jnp.float32,
            )
            out_ref[block] = jnp.maximum(projected, 0.0).astype(out_ref.dtype)


def dense_layer(row, stripe, tiles, start, weight, dtype, group=16):
    shards = stripe.shape[0]
    whole = lambda shape: pl.BlockSpec(shape, lambda at, *_: (0,) * len(shape))
    return pl.pallas_call(
        functools.partial(dense_kernel, group),
        out_shape=jax.ShapeDtypeStruct((NB, TILE, F), dtype),
        grid_spec=pltpu.PrefetchScalarGridSpec(
            num_scalar_prefetch=1,
            grid=(shards // group,),
            in_specs=[
                pl.BlockSpec((group, TILE, F), lambda at, *_: (at, 0, 0)),
                pl.BlockSpec((group, TILE, TILE), lambda at, *_: (at, 0, 0)),
                whole((TILE, NB * F)),
                whole((F, F)),
            ],
            out_specs=whole((NB, TILE, F)),
            scratch_shapes=[pltpu.VMEM((TILE, NB * F), jnp.float32)],
        ),
        name="dense_layer",
    )(row, stripe, tiles, start, weight)


def shards(
    features,
    weight_one,
    weight_two,
    dense_tiles,
    dense_row,
    hub_block,
    sparse_tiles,
    sparse_row,
    sparse_src,
    sparse_count,
    fetch_list,
):
    own_index = lax.axis_index("blk")
    offsets = neighbour_offsets()
    wanted = fetch_list.reshape(2 * HOPS)
    hub_here = lax.dynamic_index_in_dim(hub_block, own_index, 0, keepdims=False)

    def propagate(blocks, weight, dtype):
        hub_rows = jnp.where(hub_here == 0, blocks[0], blocks[1])[None]
        stripe = lax.all_gather(hub_rows, "blk", axis=0, tiled=True)
        fetched = [from_behind(blocks, "blk", -offsets[entry]) for entry in range(2 * HOPS)]
        start = sparse_sums(sparse_row, sparse_src, sparse_count, wanted, blocks, fetched, sparse_tiles)
        return dense_layer(dense_row, stripe, dense_tiles, start, weight, dtype)

    hidden = propagate(features.astype(jnp.bfloat16).reshape(NB, TILE, F), weight_one, jnp.bfloat16)
    return propagate(hidden, weight_two, jnp.float32).reshape(NB * TILE, F)


def solution(mesh):
    placed = (
        P("blk", None),
        P(),
        P(),
        P("blk", None, None),
        P("blk"),
        P(),
        P("blk", None, None),
        P("blk"),
        P("blk"),
        P("blk"),
        P("blk", None),
    )
    return jax.shard_map(
        shards, mesh=mesh, in_specs=placed, out_specs=P("blk", None), check_vma=False
    )
```

```python
import functools

import jax
import jax.numpy as jnp
from jax import lax
from jax.experimental import pallas as pl
from jax.experimental.pallas import tpu as pltpu
from jax.sharding import PartitionSpec as P

F = 128
TILE = 128
NB = 2
KS = 112
HOPS = 2
FETCH = 1
SOURCES = NB + 2 * HOPS * FETCH
NZ, NX, NY, NC = 8, 4, 4, 2
SHARDS = NZ * NX * NY * NC
SIDE = 4

SMEM = pl.BlockSpec(memory_space=pltpu.SMEM)
VMEM = pl.BlockSpec(memory_space=pltpu.VMEM)
ANY = pl.BlockSpec(memory_space=pl.ANY)


def place(index):
    return index // (NX * NY * NC), index // (NY * NC) % NX, index // NC % NY, index % NC


def index_of(z, x, y, core):
    return ((z % NZ * NX + x % NX) * NY + y % NY) * NC + core % NC


def groups_along_z():
    return [[index_of(z, x, y, core) for z in range(NZ)] for x in range(NX) for y in range(NY) for core in range(NC)]


def groups_crossways():
    return [[index_of(z, x, y, 0) for y in range(NY)] for z in range(NZ) for x in range(NX)] + [
        [index_of(z, x, y, 1) for x in range(NX)] for z in range(NZ) for y in range(NY)
    ]


def ring_step(array, by):
    pairs = []
    for index in range(SHARDS):
        z, x, y, core = place(index)
        pairs.append((index, index_of(z, x + (by if core == 0 else 0), y + (by if core == 1 else 0), core)))
    return lax.ppermute(array, "blk", pairs)


def swap_cores(array):
    return lax.ppermute(array, "blk", [(i, i ^ 1) for i in range(SHARDS)])


def swap_across(array):
    return lax.ppermute(array, "blk", [(i, (i + (1 if i % 2 else -1)) % SHARDS) for i in range(SHARDS)])


def from_behind(array, by):
    return lax.ppermute(array, "blk", [(i, (i + by) % SHARDS) for i in range(SHARDS)])


def placed_pair(block, row):
    zeros = jnp.zeros_like(block)
    return jnp.concatenate([jnp.where(row == 0, block, zeros), jnp.where(row == 0, zeros, block)], axis=1)


def enter_kernel(me_ref, hub_ref, features_ref, blocks_ref, copies_ref):
    blocks = [features_ref[b * TILE : (b + 1) * TILE].astype(jnp.bfloat16) for b in range(NB)]
    hub = jnp.where(hub_ref[me_ref[0]] == 0, blocks[0], blocks[1])
    for b in range(NB):
        blocks_ref[b] = blocks[b]
    for z in range(NZ):
        copies_ref[z] = hub


def enter(me, hub_block, features):
    return pl.pallas_call(
        enter_kernel,
        out_shape=(
            jax.ShapeDtypeStruct((NB, TILE, F), jnp.bfloat16),
            jax.ShapeDtypeStruct((NZ, TILE, F), jnp.bfloat16),
        ),
        in_specs=[SMEM, SMEM, VMEM],
        out_specs=(VMEM, VMEM),
        compiler_params=pltpu.CompilerParams(vmem_limit_bytes=8 << 20),
        name="enter",
    )(me, hub_block, features)


def sparse_kernel(me_ref, row_ref, src_ref, count_ref, fetch_ref, blocks_ref, behind_ref, swap_ref, across_ref, ahead_ref, tiles_ref, out_ref, placed_ref):
    zeros = jnp.zeros((TILE, F), jnp.bfloat16)
    even = me_ref[0] % 2 == 0
    before, after = fetch_ref[0, 1], fetch_ref[0, 2]
    blocks = [
        blocks_ref[0],
        blocks_ref[1],
        behind_ref[fetch_ref[0, 0]],
        jnp.where(even, across_ref[before], swap_ref[before]),
        jnp.where(even, swap_ref[after], across_ref[after]),
        ahead_ref[fetch_ref[0, 3]],
    ]
    for source in range(SOURCES):
        placed_ref[2 * source] = jnp.concatenate([blocks[source], zeros], axis=1)
        placed_ref[2 * source + 1] = jnp.concatenate([zeros, blocks[source]], axis=1)
    placed_ref[2 * SOURCES] = jnp.zeros((TILE, NB * F), jnp.bfloat16)
    out_ref[...] = jnp.zeros_like(out_ref)
    live = count_ref[0]

    def which(slot):
        return jnp.where(slot < live, 2 * src_ref[slot] + row_ref[slot], 2 * SOURCES)

    group = 8

    def step(at, _):
        first = at * group
        left = jnp.concatenate([tiles_ref[first + k] for k in range(group)], axis=1)
        right = jnp.concatenate([placed_ref[which(first + k)] for k in range(group)], axis=0)
        out_ref[...] += jnp.dot(left, right, preferred_element_type=jnp.float32)
        return 0

    lax.fori_loop(0, (live + group - 1) // group, step, 0)


def sparse_sums(me, row, src, count, wanted, blocks, fetched, tiles):
    return pl.pallas_call(
        sparse_kernel,
        out_shape=jax.ShapeDtypeStruct((TILE, NB * F), jnp.float32),
        in_specs=[SMEM] * 5 + [VMEM] * (2 + 2 * HOPS),
        out_specs=VMEM,
        scratch_shapes=[pltpu.VMEM((2 * SOURCES + 1, TILE, NB * F), jnp.bfloat16)],
        cost_estimate=pl.CostEstimate(flops=2 * KS * TILE**3, bytes_accessed=2 * KS * TILE**2, transcendentals=0),
        compiler_params=pltpu.CompilerParams(vmem_limit_bytes=16 << 20),
        name="sparse_sums",
    )(me, row, src, count, wanted, blocks, *fetched, tiles)


def dense_kernel(counts, me_ref, shift_ref, own_row_ref, other_row_ref, *refs):
    chunk_refs, (own_ref, other_ref, start_ref, out_ref, held, sems) = refs[: len(counts)], refs[len(counts) :]
    me = me_ref[0]
    x, y, core = me // (NY * NC) % NX, me // NC % NY, me % NC
    fixed = (jnp.where(core == 0, x, y) + shift_ref[0]) % SIDE
    origins = []
    copies = []
    for step in range(sum(counts)):
        at_x = jnp.where(core == 0, fixed, step)
        at_y = jnp.where(core == 0, step, fixed)
        origins.append((at_x * NY + at_y) * NC + core)
        for side, tiles_ref in enumerate((own_ref, other_ref)):
            copies.append(
                pltpu.make_async_copy(tiles_ref.at[:, at_x, at_y, core], held.at[step, side], sems.at[step, side])
            )
            copies[-1].start()
    out_ref[...] = start_ref[...]
    step = 0
    for chunk_ref, count in zip(chunk_refs, counts):
        for k in range(count):
            for side, row_ref in enumerate((own_row_ref, other_row_ref)):
                copies[2 * step + side].wait()
                left = jnp.concatenate([held[step, side, z] for z in range(NZ)], axis=1)
                right = jnp.concatenate(
                    [
                        placed_pair(chunk_ref[k, z], row_ref[z * (NX * NY * NC) + origins[step]])
                        for z in range(NZ)
                    ],
                    axis=0,
                )
                out_ref[side] += jnp.dot(left, right, preferred_element_type=jnp.float32)
            step += 1


def dense_part(me, shift, rows, chunks, tiles, start):
    counts = tuple(chunk.shape[0] for chunk in chunks)
    steps = sum(counts)
    return pl.pallas_call(
        functools.partial(dense_kernel, counts),
        out_shape=jax.ShapeDtypeStruct((NC, TILE, NB * F), jnp.float32),
        in_specs=[SMEM] * 4 + [VMEM] * len(chunks) + [ANY, ANY, VMEM],
        out_specs=VMEM,
        scratch_shapes=[
            pltpu.VMEM((steps, NC, NZ, TILE, TILE), jnp.bfloat16),
            pltpu.SemaphoreType.DMA((steps, NC)),
        ],
        compiler_params=pltpu.CompilerParams(vmem_limit_bytes=16 << 20),
        cost_estimate=pl.CostEstimate(
            flops=8 * steps * NZ * TILE**3, bytes_accessed=6 * steps * NZ * TILE**2, transcendentals=0
        ),
        name="dense_part",
    )(me, jnp.array([shift], jnp.int32), *rows, *chunks, *tiles, start)


def finish_kernel(wide, me_ref, hub_ref, dense_ref, other_ref, sparse_ref, weight_ref, out_ref, *copies):
    blocks = []
    for block in range(NB):
        columns = slice(block * F, (block + 1) * F)
        summed = dense_ref[0, :, columns] + other_ref[:, columns] + sparse_ref[:, columns]
        projected = jnp.dot(
            summed, weight_ref[...], precision=lax.Precision.HIGHEST, preferred_element_type=jnp.float32
        )
        blocks.append(jnp.maximum(projected, 0.0).astype(out_ref.dtype))
        out_ref[block] = blocks[block]
    if wide:
        hub = jnp.where(hub_ref[me_ref[0]] == 0, blocks[0], blocks[1])
        for z in range(NZ):
            copies[0][z] = hub


def finish(me, hub_block, dense, other, sparse, weight, dtype, wide):
    shape = jax.ShapeDtypeStruct((NB, TILE, F), dtype)
    copies = [jax.ShapeDtypeStruct((NZ, TILE, F), dtype)] if wide else []
    return pl.pallas_call(
        functools.partial(finish_kernel, wide),
        out_shape=(shape, *copies),
        in_specs=[SMEM, SMEM] + [VMEM] * 4,
        out_specs=(VMEM,) * (1 + len(copies)),
        compiler_params=pltpu.CompilerParams(vmem_limit_bytes=8 << 20),
        name="finish",
    )(me, hub_block, dense, other, sparse, weight)


def shards(
    features,
    weight_one,
    weight_two,
    dense_tiles,
    dense_row,
    hub_block,
    sparse_tiles,
    sparse_row,
    sparse_src,
    sparse_count,
    fetch_list,
):
    me = lax.axis_index("blk").astype(jnp.int32).reshape(1)
    tiles = [array.reshape(NZ, NX, NY, NC, TILE, TILE) for array in (dense_tiles, swap_cores(dense_tiles))]
    rows = [dense_row, swap_cores(dense_row)]
    zeros = jnp.zeros((NC, TILE, NB * F), jnp.float32)

    def propagate(blocks, copies, weight, dtype, wide):
        column = lax.all_to_all(copies, "blk", 0, 0, axis_index_groups=groups_along_z(), tiled=True)
        plane = lax.all_to_all(
            jnp.broadcast_to(column[None], (SIDE, NZ, TILE, F)),
            "blk",
            0,
            0,
            axis_index_groups=groups_crossways(),
            tiled=True,
        )
        blocks, plane = lax.optimization_barrier((blocks, plane))
        behind = ring_step(plane, 1)
        ahead = ring_step(plane, -1)
        fetched = [from_behind(blocks, 2), swap_cores(blocks), swap_across(blocks), from_behind(blocks, -2)]
        total = dense_part(me, 0, rows, [plane], tiles, zeros)
        behind, ahead, total = lax.optimization_barrier((behind, ahead, total))
        far = (ring_step(behind[: SIDE // 2], 1), ring_step(ahead[SIDE // 2 :], -1))
        total = dense_part(me, SIDE - 1, rows, [behind], tiles, total)
        total = dense_part(me, 1, rows, [ahead], tiles, total)
        sparse = sparse_sums(me, sparse_row, sparse_src, sparse_count, fetch_list, blocks, fetched, sparse_tiles)
        far, total, sparse = lax.optimization_barrier((far, total, sparse))
        total = dense_part(me, 2, rows, far, tiles, total)
        returned = swap_cores(total[1])
        return finish(me, hub_block, total, returned, sparse, weight, dtype, wide)

    blocks, copies = enter(me, hub_block, features)
    hidden, copies = propagate(blocks, copies, weight_one, jnp.bfloat16, True)
    (embedded,) = propagate(hidden, copies, weight_two, jnp.float32, False)
    return embedded.reshape(NB * TILE, F)


def solution(mesh):
    placed = (
        P("blk", None),
        P(),
        P(),
        P("blk", None, None),
        P("blk"),
        P(),
        P("blk", None, None),
        P("blk"),
        P("blk"),
        P("blk"),
        P("blk", None),
    )
    return jax.shard_map(
        shards, mesh=mesh, in_specs=placed, out_specs=P("blk", None), check_vma=False
    )
```

```python
import functools

import jax
import jax.numpy as jnp
from jax import lax
from jax.experimental import pallas as pl
from jax.experimental.pallas import tpu as pltpu
from jax.sharding import PartitionSpec as P


F = 128
TILE = 128
NB = 2
KS = 112
HOPS = 2
FETCH = 1
SOURCES = NB + 2 * HOPS * FETCH
NZ, NX, NY, NC = 8, 4, 4, 2
SHARDS = NZ * NX * NY * NC
SIDE = 4

SMEM = pl.BlockSpec(memory_space=pltpu.SMEM)
VMEM = pl.BlockSpec(memory_space=pltpu.VMEM)
HBM = pl.BlockSpec(memory_space=pltpu.HBM)


def place(index):
    return index // (NX * NY * NC), index // (NY * NC) % NX, index // NC % NY, index % NC


def index_of(z, x, y, core):
    return ((z % NZ * NX + x % NX) * NY + y % NY) * NC + core % NC


def groups_along_z():
    return [[index_of(z, x, y, core) for z in range(NZ)] for x in range(NX) for y in range(NY) for core in range(NC)]


def groups_crossways():
    return [[index_of(z, x, y, 0) for y in range(NY)] for z in range(NZ) for x in range(NX)] + [
        [index_of(z, x, y, 1) for x in range(NX)] for z in range(NZ) for y in range(NY)
    ]


def ring_step(array, by):
    pairs = []
    for index in range(SHARDS):
        z, x, y, core = place(index)
        pairs.append((index, index_of(z, x + (by if core == 0 else 0), y + (by if core == 1 else 0), core)))
    return lax.ppermute(array, "blk", pairs)


def swap_cores(array):
    return lax.ppermute(array, "blk", [(i, i ^ 1) for i in range(SHARDS)])


def swap_across(array):
    return lax.ppermute(array, "blk", [(i, (i + (1 if i % 2 else -1)) % SHARDS) for i in range(SHARDS)])


def from_behind(array, by):
    return lax.ppermute(array, "blk", [(i, (i + by) % SHARDS) for i in range(SHARDS)])


def placed_pair(block, row):
    zeros = jnp.zeros_like(block)
    return jnp.concatenate([jnp.where(row == 0, block, zeros), jnp.where(row == 0, zeros, block)], axis=1)


def enter_kernel(me_ref, hub_ref, features_ref, blocks_ref, copies_ref):
    blocks = [features_ref[b * TILE : (b + 1) * TILE].astype(jnp.bfloat16) for b in range(NB)]
    hub = jnp.where(hub_ref[me_ref[0]] == 0, blocks[0], blocks[1])
    for b in range(NB):
        blocks_ref[b] = blocks[b]
    for z in range(NZ):
        copies_ref[z] = hub


def enter(me, hub_block, features):
    return pl.pallas_call(
        enter_kernel,
        out_shape=(
            jax.ShapeDtypeStruct((NB, TILE, F), jnp.bfloat16),
            jax.ShapeDtypeStruct((NZ, TILE, F), jnp.bfloat16),
        ),
        in_specs=[SMEM, SMEM, VMEM],
        out_specs=(VMEM, VMEM),
        compiler_params=pltpu.CompilerParams(vmem_limit_bytes=8 << 20),
        name="enter",
    )(me, hub_block, features)


def sparse_kernel(me_ref, row_ref, src_ref, count_ref, fetch_ref, blocks_ref, behind_ref, swap_ref, across_ref, ahead_ref, tiles_ref, out_ref, placed_ref):
    zeros = jnp.zeros((TILE, F), jnp.bfloat16)
    even = me_ref[0] % 2 == 0
    before, after = fetch_ref[0, 1], fetch_ref[0, 2]
    blocks = [
        blocks_ref[0],
        blocks_ref[1],
        behind_ref[fetch_ref[0, 0]],
        jnp.where(even, across_ref[before], swap_ref[before]),
        jnp.where(even, swap_ref[after], across_ref[after]),
        ahead_ref[fetch_ref[0, 3]],
    ]
    for source in range(SOURCES):
        placed_ref[2 * source] = jnp.concatenate([blocks[source], zeros], axis=1)
        placed_ref[2 * source + 1] = jnp.concatenate([zeros, blocks[source]], axis=1)
    placed_ref[2 * SOURCES] = jnp.zeros((TILE, NB * F), jnp.bfloat16)
    out_ref[...] = jnp.zeros_like(out_ref)
    live = count_ref[0]

    def which(slot):
        return jnp.where(slot < live, 2 * src_ref[slot] + row_ref[slot], 2 * SOURCES)

    group = 8

    def step(at, _):
        first = at * group
        left = jnp.concatenate([tiles_ref[first + k] for k in range(group)], axis=1)
        right = jnp.concatenate([placed_ref[which(first + k)] for k in range(group)], axis=0)
        out_ref[...] += jnp.dot(left, right, preferred_element_type=jnp.float32)
        return 0

    lax.fori_loop(0, (live + group - 1) // group, step, 0)


def sparse_sums(me, row, src, count, wanted, blocks, fetched, tiles):
    return pl.pallas_call(
        sparse_kernel,
        out_shape=jax.ShapeDtypeStruct((TILE, NB * F), jnp.float32),
        in_specs=[SMEM] * 5 + [VMEM] * (2 + 2 * HOPS),
        out_specs=VMEM,
        scratch_shapes=[pltpu.VMEM((2 * SOURCES + 1, TILE, NB * F), jnp.bfloat16)],
        cost_estimate=pl.CostEstimate(flops=2 * KS * TILE**3, bytes_accessed=2 * KS * TILE**2, transcendentals=0),
        compiler_params=pltpu.CompilerParams(vmem_limit_bytes=16 << 20),
        name="sparse_sums",
    )(me, row, src, count, wanted, blocks, *fetched, tiles)


def collect_kernel(me_ref, own_ref, other_ref, out_ref, sems):
    core = me_ref[0] % NC
    copies = [
        pltpu.make_async_copy(tiles_ref.at[z, :, :, core], out_ref.at[side, z], sems.at[side, z])
        for side, tiles_ref in enumerate((own_ref, other_ref))
        for z in range(NZ)
    ]
    for copy in copies:
        copy.start()
    for copy in copies:
        copy.wait()


def collect(me, own, other):
    shape = (NZ, NX, NY, NC, TILE, TILE)
    return pl.pallas_call(
        collect_kernel,
        out_shape=jax.ShapeDtypeStruct((NC, NZ, NX, NY, TILE, TILE), jnp.bfloat16),
        in_specs=[SMEM, HBM, HBM],
        out_specs=VMEM,
        scratch_shapes=[pltpu.SemaphoreType.DMA((NC, NZ))],
        compiler_params=pltpu.CompilerParams(vmem_limit_bytes=12 << 20),
        cost_estimate=pl.CostEstimate(flops=0, bytes_accessed=2 * SHARDS * TILE**2, transcendentals=0),
        name="collect",
    )(me, own.reshape(shape), other.reshape(shape))


def dense_kernel(counts, me_ref, shift_ref, own_row_ref, other_row_ref, *refs):
    chunk_refs, (tiles_ref, start_ref, out_ref) = refs[: len(counts)], refs[len(counts) :]
    me = me_ref[0]
    x, y, core = me // (NY * NC) % NX, me // NC % NY, me % NC
    fixed = (jnp.where(core == 0, x, y) + shift_ref[0]) % SIDE
    out_ref[...] = start_ref[...]
    step = 0
    for chunk_ref, count in zip(chunk_refs, counts):
        for k in range(count):
            at_x = jnp.where(core == 0, fixed, step)
            at_y = jnp.where(core == 0, step, fixed)
            sources = [((z * NX + at_x) * NY + at_y) * NC + core for z in range(NZ)]
            for side, row_ref in enumerate((own_row_ref, other_row_ref)):
                left = jnp.concatenate([tiles_ref[side, z, at_x, at_y] for z in range(NZ)], axis=1)
                right = jnp.concatenate(
                    [placed_pair(chunk_ref[k, z], row_ref[source]) for z, source in enumerate(sources)], axis=0
                )
                out_ref[side] += jnp.dot(left, right, preferred_element_type=jnp.float32)
            step += 1


def dense_part(me, shift, rows, chunks, tiles, start):
    counts = tuple(chunk.shape[0] for chunk in chunks)
    steps = sum(counts)
    return pl.pallas_call(
        functools.partial(dense_kernel, counts),
        out_shape=jax.ShapeDtypeStruct((NC, TILE, NB * F), jnp.float32),
        in_specs=[SMEM] * 4 + [VMEM] * (len(chunks) + 2),
        out_specs=VMEM,
        compiler_params=pltpu.CompilerParams(vmem_limit_bytes=16 << 20),
        cost_estimate=pl.CostEstimate(
            flops=8 * steps * NZ * TILE**3, bytes_accessed=6 * steps * NZ * TILE**2, transcendentals=0
        ),
        name="dense_part",
    )(me, jnp.array([shift], jnp.int32), *rows, *chunks, tiles, start)


def finish_kernel(wide, me_ref, hub_ref, dense_ref, other_ref, sparse_ref, weight_ref, out_ref, *copies):
    blocks = []
    for block in range(NB):
        columns = slice(block * F, (block + 1) * F)
        summed = dense_ref[0, :, columns] + other_ref[:, columns] + sparse_ref[:, columns]
        projected = jnp.dot(
            summed, weight_ref[...], precision=lax.Precision.HIGHEST, preferred_element_type=jnp.float32
        )
        blocks.append(jnp.maximum(projected, 0.0).astype(out_ref.dtype))
        out_ref[block] = blocks[block]
    if wide:
        hub = jnp.where(hub_ref[me_ref[0]] == 0, blocks[0], blocks[1])
        for z in range(NZ):
            copies[0][z] = hub


def finish(me, hub_block, dense, other, sparse, weight, dtype, wide):
    shape = jax.ShapeDtypeStruct((NB, TILE, F), dtype)
    copies = [jax.ShapeDtypeStruct((NZ, TILE, F), dtype)] if wide else []
    return pl.pallas_call(
        functools.partial(finish_kernel, wide),
        out_shape=(shape, *copies),
        in_specs=[SMEM, SMEM] + [VMEM] * 4,
        out_specs=(VMEM,) * (1 + len(copies)),
        compiler_params=pltpu.CompilerParams(vmem_limit_bytes=8 << 20),
        name="finish",
    )(me, hub_block, dense, other, sparse, weight)


def shards(
    features,
    weight_one,
    weight_two,
    dense_tiles,
    dense_row,
    hub_block,
    sparse_tiles,
    sparse_row,
    sparse_src,
    sparse_count,
    fetch_list,
):
    me = lax.axis_index("blk").astype(jnp.int32).reshape(1)
    rows = [dense_row, swap_cores(dense_row)]
    other_tiles = swap_cores(dense_tiles)
    zeros = jnp.zeros((NC, TILE, NB * F), jnp.float32)

    def propagate(blocks, copies, weight, dtype, wide, tiles=None):
        column = lax.all_to_all(copies, "blk", 0, 0, axis_index_groups=groups_along_z(), tiled=True)
        plane = lax.all_to_all(
            jnp.broadcast_to(column[None], (SIDE, NZ, TILE, F)),
            "blk",
            0,
            0,
            axis_index_groups=groups_crossways(),
            tiled=True,
        )
        if tiles is None:
            blocks, plane, others = lax.optimization_barrier((blocks, plane, other_tiles))
            tiles = collect(me, dense_tiles, others)
        else:
            blocks, plane = lax.optimization_barrier((blocks, plane))
        behind = ring_step(plane, 1)
        ahead = ring_step(plane, -1)
        fetched = [from_behind(blocks, 2), swap_cores(blocks), swap_across(blocks), from_behind(blocks, -2)]
        total = dense_part(me, 0, rows, [plane], tiles, zeros)
        behind, ahead, total = lax.optimization_barrier((behind, ahead, total))
        far = (ring_step(behind[: SIDE // 2], 1), ring_step(ahead[SIDE // 2 :], -1))
        total = dense_part(me, SIDE - 1, rows, [behind], tiles, total)
        total = dense_part(me, 1, rows, [ahead], tiles, total)
        sparse = sparse_sums(me, sparse_row, sparse_src, sparse_count, fetch_list, blocks, fetched, sparse_tiles)
        far, total, sparse = lax.optimization_barrier((far, total, sparse))
        total = dense_part(me, 2, rows, far, tiles, total)
        returned = swap_cores(total[1])
        return *finish(me, hub_block, total, returned, sparse, weight, dtype, wide), tiles

    blocks, copies = enter(me, hub_block, features)
    hidden, copies, tiles = propagate(blocks, copies, weight_one, jnp.bfloat16, True)
    embedded, _ = propagate(hidden, copies, weight_two, jnp.float32, False, tiles)
    return embedded.reshape(NB * TILE, F)


def solution(mesh):
    placed = (
        P("blk", None),
        P(),
        P(),
        P("blk", None, None),
        P("blk"),
        P(),
        P("blk", None, None),
        P("blk"),
        P("blk"),
        P("blk"),
        P("blk", None),
    )
    return jax.shard_map(shards, mesh=mesh, in_specs=placed, out_specs=P("blk", None), check_vma=False)
```

```python
import functools

import jax
import jax.numpy as jnp
from jax import lax
from jax.experimental import pallas as pl
from jax.experimental.pallas import tpu as pltpu
from jax.sharding import PartitionSpec as P


F = 128
TILE = 128
NB = 2
KS = 112
HOPS = 2
FETCH = 1
SOURCES = NB + 2 * HOPS * FETCH
NZ, NX, NY, NC = 8, 4, 4, 2
SHARDS = NZ * NX * NY * NC
SIDE = 4
TURNS = (0, SIDE - 1, 1, 2)

SMEM = pl.BlockSpec(memory_space=pltpu.SMEM)
VMEM = pl.BlockSpec(memory_space=pltpu.VMEM)
HBM = pl.BlockSpec(memory_space=pltpu.HBM)


def place(index):
    return index // (NX * NY * NC), index // (NY * NC) % NX, index // NC % NY, index % NC


def index_of(z, x, y, core):
    return ((z % NZ * NX + x % NX) * NY + y % NY) * NC + core % NC


def groups_along_z():
    return [[index_of(z, x, y, core) for z in range(NZ)] for x in range(NX) for y in range(NY) for core in range(NC)]


def step(array, by, across):
    pairs = []
    for index in range(SHARDS):
        z, x, y, core = place(index)
        along_x = (core == 0) != across
        pairs.append((index, index_of(z, x + (by if along_x else 0), y + (0 if along_x else by), core)))
    return lax.ppermute(array, "blk", pairs)


def swap_cores(array):
    return lax.ppermute(array, "blk", [(i, i ^ 1) for i in range(SHARDS)])


def swap_across(array):
    return lax.ppermute(array, "blk", [(i, (i + (1 if i % 2 else -1)) % SHARDS) for i in range(SHARDS)])


def from_behind(array, by):
    return lax.ppermute(array, "blk", [(i, (i + by) % SHARDS) for i in range(SHARDS)])


def placed_pair(block, row):
    zeros = jnp.zeros_like(block)
    return jnp.concatenate([jnp.where(row == 0, block, zeros), jnp.where(row == 0, zeros, block)], axis=1)


def enter_kernel(me_ref, hub_ref, features_ref, blocks_ref, copies_ref):
    blocks = [features_ref[b * TILE : (b + 1) * TILE].astype(jnp.bfloat16) for b in range(NB)]
    hub = jnp.where(hub_ref[me_ref[0]] == 0, blocks[0], blocks[1])
    for b in range(NB):
        blocks_ref[b] = blocks[b]
    for z in range(NZ):
        copies_ref[z] = hub


def enter(me, hub_block, features):
    return pl.pallas_call(
        enter_kernel,
        out_shape=(
            jax.ShapeDtypeStruct((NB, TILE, F), jnp.bfloat16),
            jax.ShapeDtypeStruct((NZ, TILE, F), jnp.bfloat16),
        ),
        in_specs=[SMEM, SMEM, VMEM],
        out_specs=(VMEM, VMEM),
        compiler_params=pltpu.CompilerParams(vmem_limit_bytes=8 << 20),
        name="enter",
    )(me, hub_block, features)


def sparse_kernel(me_ref, row_ref, src_ref, count_ref, fetch_ref, blocks_ref, behind_ref, swap_ref, across_ref, ahead_ref, tiles_ref, out_ref, placed_ref):
    zeros = jnp.zeros((TILE, F), jnp.bfloat16)
    even = me_ref[0] % 2 == 0
    before, after = fetch_ref[0, 1], fetch_ref[0, 2]
    blocks = [
        blocks_ref[0],
        blocks_ref[1],
        behind_ref[fetch_ref[0, 0]],
        jnp.where(even, across_ref[before], swap_ref[before]),
        jnp.where(even, swap_ref[after], across_ref[after]),
        ahead_ref[fetch_ref[0, 3]],
    ]
    for source in range(SOURCES):
        placed_ref[2 * source] = jnp.concatenate([blocks[source], zeros], axis=1)
        placed_ref[2 * source + 1] = jnp.concatenate([zeros, blocks[source]], axis=1)
    placed_ref[2 * SOURCES] = jnp.zeros((TILE, NB * F), jnp.bfloat16)
    out_ref[...] = jnp.zeros_like(out_ref)
    live = count_ref[0]

    def which(slot):
        return jnp.where(slot < live, 2 * src_ref[slot] + row_ref[slot], 2 * SOURCES)

    group = 8

    def add(at, _):
        first = at * group
        left = jnp.concatenate([tiles_ref[first + k] for k in range(group)], axis=1)
        right = jnp.concatenate([placed_ref[which(first + k)] for k in range(group)], axis=0)
        out_ref[...] += jnp.dot(left, right, preferred_element_type=jnp.float32)
        return 0

    lax.fori_loop(0, (live + group - 1) // group, add, 0)


def sparse_sums(me, row, src, count, wanted, blocks, fetched, tiles):
    return pl.pallas_call(
        sparse_kernel,
        out_shape=jax.ShapeDtypeStruct((TILE, NB * F), jnp.float32),
        in_specs=[SMEM] * 5 + [VMEM] * (2 + 2 * HOPS),
        out_specs=VMEM,
        scratch_shapes=[pltpu.VMEM((2 * SOURCES + 1, TILE, NB * F), jnp.bfloat16)],
        cost_estimate=pl.CostEstimate(flops=2 * KS * TILE**3, bytes_accessed=2 * KS * TILE**2, transcendentals=0),
        compiler_params=pltpu.CompilerParams(vmem_limit_bytes=16 << 20),
        name="sparse_sums",
    )(me, row, src, count, wanted, blocks, *fetched, tiles)


def collect_kernel(me_ref, own_ref, other_ref, out_ref, sems):
    core = me_ref[0] % NC
    copies = [
        pltpu.make_async_copy(tiles_ref.at[z, :, :, core], out_ref.at[side, z], sems.at[side, z])
        for side, tiles_ref in enumerate((own_ref, other_ref))
        for z in range(NZ)
    ]
    for copy in copies:
        copy.start()
    for copy in copies:
        copy.wait()


def collect(me, own, other):
    shape = (NZ, NX, NY, NC, TILE, TILE)
    return pl.pallas_call(
        collect_kernel,
        out_shape=jax.ShapeDtypeStruct((NC, NZ, NX, NY, TILE, TILE), jnp.bfloat16),
        in_specs=[SMEM, HBM, HBM],
        out_specs=VMEM,
        scratch_shapes=[pltpu.SemaphoreType.DMA((NC, NZ))],
        compiler_params=pltpu.CompilerParams(vmem_limit_bytes=12 << 20),
        cost_estimate=pl.CostEstimate(flops=0, bytes_accessed=2 * SHARDS * TILE**2, transcendentals=0),
        name="collect",
    )(me, own.reshape(shape), other.reshape(shape))


def dense_kernel(sides, me_ref, shift_ref, *refs):
    count = len(sides)
    row_refs, (chunk_ref, tiles_ref), start_refs, out_refs = refs[:count], refs[count : count + 2], refs[count + 2 : -count], refs[-count:]
    me = me_ref[0]
    x, y, core = me // (NY * NC) % NX, me // NC % NY, me % NC
    fixed = (jnp.where(core == 0, x, y) + shift_ref[0]) % SIDE
    for start_ref, out_ref in zip(start_refs, out_refs):
        out_ref[...] = start_ref[...]
    for k, turn in enumerate(TURNS):
        along = (jnp.where(core == 0, y, x) + turn) % SIDE
        at_x = jnp.where(core == 0, fixed, along)
        at_y = jnp.where(core == 0, along, fixed)
        sources = [((z * NX + at_x) * NY + at_y) * NC + core for z in range(NZ)]
        for side, row_ref, out_ref in zip(sides, row_refs, out_refs):
            left = jnp.concatenate([tiles_ref[side, z, at_x, at_y] for z in range(NZ)], axis=1)
            right = jnp.concatenate(
                [placed_pair(chunk_ref[k, z], row_ref[source]) for z, source in enumerate(sources)], axis=0
            )
            out_ref[...] += jnp.dot(left, right, preferred_element_type=jnp.float32)


def dense_part(me, shift, rows, chunk, tiles, starts, sides=(0, 1)):
    count = len(sides)
    return pl.pallas_call(
        functools.partial(dense_kernel, sides),
        out_shape=(jax.ShapeDtypeStruct((TILE, NB * F), jnp.float32),) * count,
        in_specs=[SMEM] * (2 + count) + [VMEM] * (2 + count),
        out_specs=(VMEM,) * count,
        compiler_params=pltpu.CompilerParams(vmem_limit_bytes=16 << 20),
        cost_estimate=pl.CostEstimate(
            flops=4 * count * SIDE * NZ * TILE**3, bytes_accessed=3 * count * SIDE * NZ * TILE**2, transcendentals=0
        ),
        name="dense_part",
    )(me, jnp.array([shift], jnp.int32), *(rows[side] for side in sides), chunk, tiles, *starts)


def finish_kernel(wide, me_ref, hub_ref, dense_ref, other_ref, sparse_ref, weight_ref, out_ref, *copies):
    blocks = []
    for block in range(NB):
        columns = slice(block * F, (block + 1) * F)
        summed = dense_ref[:, columns] + other_ref[:, columns] + sparse_ref[:, columns]
        projected = jnp.dot(
            summed, weight_ref[...], precision=lax.Precision.HIGHEST, preferred_element_type=jnp.float32
        )
        blocks.append(jnp.maximum(projected, 0.0).astype(out_ref.dtype))
        out_ref[block] = blocks[block]
    if wide:
        hub = jnp.where(hub_ref[me_ref[0]] == 0, blocks[0], blocks[1])
        for z in range(NZ):
            copies[0][z] = hub


def finish(me, hub_block, dense, other, sparse, weight, dtype, wide):
    shape = jax.ShapeDtypeStruct((NB, TILE, F), dtype)
    copies = [jax.ShapeDtypeStruct((NZ, TILE, F), dtype)] if wide else []
    return pl.pallas_call(
        functools.partial(finish_kernel, wide),
        out_shape=(shape, *copies),
        in_specs=[SMEM, SMEM] + [VMEM] * 4,
        out_specs=(VMEM,) * (1 + len(copies)),
        compiler_params=pltpu.CompilerParams(vmem_limit_bytes=8 << 20),
        name="finish",
    )(me, hub_block, dense, other, sparse, weight)


def shards(
    features,
    weight_one,
    weight_two,
    dense_tiles,
    dense_row,
    hub_block,
    sparse_tiles,
    sparse_row,
    sparse_src,
    sparse_count,
    fetch_list,
):
    me = lax.axis_index("blk").astype(jnp.int32).reshape(1)
    rows = [dense_row, swap_cores(dense_row)]
    other_tiles = swap_cores(dense_tiles)
    zeros = jnp.zeros((TILE, NB * F), jnp.float32)

    def propagate(blocks, copies, weight, dtype, wide, tiles=None):
        column = lax.all_to_all(copies, "blk", 0, 0, axis_index_groups=groups_along_z(), tiled=True)
        sides = [step(column, 1, True), step(column, -1, True), step(column, 2, True)]
        plane = jnp.stack([column, *sides])
        if tiles is None:
            blocks, plane, others = lax.optimization_barrier((blocks, plane, other_tiles))
            tiles = collect(me, dense_tiles, others)
        else:
            blocks, plane = lax.optimization_barrier((blocks, plane))
        behind = step(plane, 1, False)
        ahead = step(plane, -1, False)
        far = step(plane, 2, False)
        fetched = [from_behind(blocks, 2), swap_cores(blocks), swap_across(blocks), from_behind(blocks, -2)]
        totals = dense_part(me, 0, rows, plane, tiles, (zeros, zeros))
        sparse = sparse_sums(me, sparse_row, sparse_src, sparse_count, fetch_list, blocks, fetched, sparse_tiles)
        totals = dense_part(me, SIDE - 1, rows, behind, tiles, totals)
        totals = dense_part(me, 1, rows, ahead, tiles, totals)
        far, own, other, sparse = lax.optimization_barrier((far, *totals, sparse))
        (other,) = dense_part(me, 2, rows, far, tiles, (other,), (1,))
        returned = swap_cores(other)
        (total,) = dense_part(me, 2, rows, far, tiles, (own,), (0,))
        return *finish(me, hub_block, total, returned, sparse, weight, dtype, wide), tiles

    blocks, copies = enter(me, hub_block, features)
    hidden, copies, tiles = propagate(blocks, copies, weight_one, jnp.bfloat16, True)
    embedded, _ = propagate(hidden, copies, weight_two, jnp.float32, False, tiles)
    return embedded.reshape(NB * TILE, F)


def solution(mesh):
    placed = (
        P("blk", None),
        P(),
        P(),
        P("blk", None, None),
        P("blk"),
        P(),
        P("blk", None, None),
        P("blk"),
        P("blk"),
        P("blk"),
        P("blk", None),
    )
    return jax.shard_map(shards, mesh=mesh, in_specs=placed, out_specs=P("blk", None), check_vma=False)
```

```python
import functools

import jax
import jax.numpy as jnp
from jax import lax
from jax.experimental import pallas as pl
from jax.experimental.pallas import tpu as pltpu
from jax.sharding import PartitionSpec as P


F = 128
TILE = 128
NB = 2
KS = 112
HOPS = 2
FETCH = 1
SOURCES = NB + 2 * HOPS * FETCH
NZ, NX, NY, NC = 8, 4, 4, 2
SHARDS = NZ * NX * NY * NC
SIDE = 4
TURNS = (0, SIDE - 1, 1, 2)

SMEM = pl.BlockSpec(memory_space=pltpu.SMEM)
VMEM = pl.BlockSpec(memory_space=pltpu.VMEM)
HBM = pl.BlockSpec(memory_space=pltpu.HBM)


def place(index):
    return index // (NX * NY * NC), index // (NY * NC) % NX, index // NC % NY, index % NC


def index_of(z, x, y, core):
    return ((z % NZ * NX + x % NX) * NY + y % NY) * NC + core % NC


def groups_along_z():
    return [[index_of(z, x, y, core) for z in range(NZ)] for x in range(NX) for y in range(NY) for core in range(NC)]


def step(array, by, across):
    pairs = []
    for index in range(SHARDS):
        z, x, y, core = place(index)
        along_x = (core == 0) != across
        pairs.append((index, index_of(z, x + (by if along_x else 0), y + (0 if along_x else by), core)))
    return lax.ppermute(array, "blk", pairs)


def swap_cores(array):
    return lax.ppermute(array, "blk", [(i, i ^ 1) for i in range(SHARDS)])


def swap_across(array):
    return lax.ppermute(array, "blk", [(i, (i + (1 if i % 2 else -1)) % SHARDS) for i in range(SHARDS)])


def from_behind(array, by):
    return lax.ppermute(array, "blk", [(i, (i + by) % SHARDS) for i in range(SHARDS)])


def placed_pair(block, row):
    zeros = jnp.zeros_like(block)
    return jnp.concatenate([jnp.where(row == 0, block, zeros), jnp.where(row == 0, zeros, block)], axis=1)


def enter_kernel(me_ref, hub_ref, features_ref, blocks_ref, copies_ref):
    blocks = [features_ref[b * TILE : (b + 1) * TILE].astype(jnp.bfloat16) for b in range(NB)]
    hub = jnp.where(hub_ref[me_ref[0]] == 0, blocks[0], blocks[1])
    for b in range(NB):
        blocks_ref[b] = blocks[b]
    for z in range(NZ):
        copies_ref[z] = hub


def enter(me, hub_block, features):
    return pl.pallas_call(
        enter_kernel,
        out_shape=(
            jax.ShapeDtypeStruct((NB, TILE, F), jnp.bfloat16),
            jax.ShapeDtypeStruct((NZ, TILE, F), jnp.bfloat16),
        ),
        in_specs=[SMEM, SMEM, VMEM],
        out_specs=(VMEM, VMEM),
        compiler_params=pltpu.CompilerParams(vmem_limit_bytes=8 << 20),
        name="enter",
    )(me, hub_block, features)


def sparse_kernel(me_ref, row_ref, src_ref, count_ref, fetch_ref, blocks_ref, behind_ref, swap_ref, across_ref, ahead_ref, tiles_ref, out_ref, placed_ref):
    zeros = jnp.zeros((TILE, F), jnp.bfloat16)
    even = me_ref[0] % 2 == 0
    before, after = fetch_ref[0, 1], fetch_ref[0, 2]
    blocks = [
        blocks_ref[0],
        blocks_ref[1],
        behind_ref[fetch_ref[0, 0]],
        jnp.where(even, across_ref[before], swap_ref[before]),
        jnp.where(even, swap_ref[after], across_ref[after]),
        ahead_ref[fetch_ref[0, 3]],
    ]
    for source in range(SOURCES):
        placed_ref[2 * source] = jnp.concatenate([blocks[source], zeros], axis=1)
        placed_ref[2 * source + 1] = jnp.concatenate([zeros, blocks[source]], axis=1)
    placed_ref[2 * SOURCES] = jnp.zeros((TILE, NB * F), jnp.bfloat16)
    out_ref[...] = jnp.zeros_like(out_ref)
    live = count_ref[0]

    def which(slot):
        return jnp.where(slot < live, 2 * src_ref[slot] + row_ref[slot], 2 * SOURCES)

    group = 8

    def add(at, _):
        first = at * group
        left = jnp.concatenate([tiles_ref[first + k] for k in range(group)], axis=1)
        right = jnp.concatenate([placed_ref[which(first + k)] for k in range(group)], axis=0)
        out_ref[...] += jnp.dot(left, right, preferred_element_type=jnp.float32)
        return 0

    lax.fori_loop(0, (live + group - 1) // group, add, 0)


def sparse_sums(me, row, src, count, wanted, blocks, fetched, tiles):
    return pl.pallas_call(
        sparse_kernel,
        out_shape=jax.ShapeDtypeStruct((TILE, NB * F), jnp.float32),
        in_specs=[SMEM] * 5 + [VMEM] * (2 + 2 * HOPS),
        out_specs=VMEM,
        scratch_shapes=[pltpu.VMEM((2 * SOURCES + 1, TILE, NB * F), jnp.bfloat16)],
        cost_estimate=pl.CostEstimate(flops=2 * KS * TILE**3, bytes_accessed=2 * KS * TILE**2, transcendentals=0),
        compiler_params=pltpu.CompilerParams(vmem_limit_bytes=16 << 20),
        name="sparse_sums",
    )(me, row, src, count, wanted, blocks, *fetched, tiles)


def collect_kernel(me_ref, own_ref, other_ref, out_ref, sems):
    core = me_ref[0] % NC
    copies = [
        pltpu.make_async_copy(tiles_ref.at[z, :, :, core], out_ref.at[side, z], sems.at[side, z])
        for side, tiles_ref in enumerate((own_ref, other_ref))
        for z in range(NZ)
    ]
    for copy in copies:
        copy.start()
    for copy in copies:
        copy.wait()


def collect(me, own, other):
    shape = (NZ, NX, NY, NC, TILE, TILE)
    return pl.pallas_call(
        collect_kernel,
        out_shape=jax.ShapeDtypeStruct((NC, NZ, NX, NY, TILE, TILE), jnp.bfloat16),
        in_specs=[SMEM, HBM, HBM],
        out_specs=VMEM,
        scratch_shapes=[pltpu.SemaphoreType.DMA((NC, NZ))],
        compiler_params=pltpu.CompilerParams(vmem_limit_bytes=44 << 20),
        cost_estimate=pl.CostEstimate(flops=0, bytes_accessed=2 * SHARDS * TILE**2, transcendentals=0),
        name="collect",
    )(me, own.reshape(shape), other.reshape(shape))


def dense_kernel(halves, me_ref, shift_ref, own_row_ref, other_row_ref, *refs):
    chunk_refs, (tiles_ref, start_ref, out_ref) = refs[:halves], refs[halves:]
    me = me_ref[0]
    x, y, core = me // (NY * NC) % NX, me // NC % NY, me % NC
    fixed = (jnp.where(core == 0, x, y) + shift_ref[0]) % SIDE
    out_ref[...] = start_ref[...]
    for k, turn in enumerate(TURNS):
        chunk_ref, at = chunk_refs[k * halves // SIDE], k % (SIDE // halves)
        along = (jnp.where(core == 0, y, x) + turn) % SIDE
        at_x = jnp.where(core == 0, fixed, along)
        at_y = jnp.where(core == 0, along, fixed)
        sources = [((z * NX + at_x) * NY + at_y) * NC + core for z in range(NZ)]
        for side, row_ref in enumerate((own_row_ref, other_row_ref)):
            left = jnp.concatenate([tiles_ref[side, z, at_x, at_y] for z in range(NZ)], axis=1)
            right = jnp.concatenate(
                [placed_pair(chunk_ref[at, z], row_ref[source]) for z, source in enumerate(sources)], axis=0
            )
            out_ref[side] += jnp.dot(left, right, preferred_element_type=jnp.float32)


def dense_part(me, shift, rows, chunks, tiles, start):
    return pl.pallas_call(
        functools.partial(dense_kernel, len(chunks)),
        out_shape=jax.ShapeDtypeStruct((NC, TILE, NB * F), jnp.float32),
        in_specs=[SMEM] * 4 + [VMEM] * (len(chunks) + 2),
        out_specs=VMEM,
        compiler_params=pltpu.CompilerParams(vmem_limit_bytes=16 << 20),
        cost_estimate=pl.CostEstimate(
            flops=8 * SIDE * NZ * TILE**3, bytes_accessed=6 * SIDE * NZ * TILE**2, transcendentals=0
        ),
        name="dense_part",
    )(me, jnp.array([shift], jnp.int32), *rows, *chunks, tiles, start)


def finish_kernel(wide, me_ref, hub_ref, dense_ref, other_ref, sparse_ref, weight_ref, out_ref, *copies):
    blocks = []
    for block in range(NB):
        columns = slice(block * F, (block + 1) * F)
        summed = dense_ref[0, :, columns] + other_ref[:, columns] + sparse_ref[:, columns]
        projected = jnp.dot(
            summed, weight_ref[...], precision=lax.Precision.HIGHEST, preferred_element_type=jnp.float32
        )
        blocks.append(jnp.maximum(projected, 0.0).astype(out_ref.dtype))
        out_ref[block] = blocks[block]
    if wide:
        hub = jnp.where(hub_ref[me_ref[0]] == 0, blocks[0], blocks[1])
        for z in range(NZ):
            copies[0][z] = hub


def finish(me, hub_block, dense, other, sparse, weight, dtype, wide):
    shape = jax.ShapeDtypeStruct((NB, TILE, F), dtype)
    copies = [jax.ShapeDtypeStruct((NZ, TILE, F), dtype)] if wide else []
    return pl.pallas_call(
        functools.partial(finish_kernel, wide),
        out_shape=(shape, *copies),
        in_specs=[SMEM, SMEM] + [VMEM] * 4,
        out_specs=(VMEM,) * (1 + len(copies)),
        compiler_params=pltpu.CompilerParams(vmem_limit_bytes=8 << 20),
        name="finish",
    )(me, hub_block, dense, other, sparse, weight)


def shards(
    features,
    weight_one,
    weight_two,
    dense_tiles,
    dense_row,
    hub_block,
    sparse_tiles,
    sparse_row,
    sparse_src,
    sparse_count,
    fetch_list,
):
    me = lax.axis_index("blk").astype(jnp.int32).reshape(1)
    rows = [dense_row, swap_cores(dense_row)]
    other_tiles = swap_cores(dense_tiles)
    zeros = jnp.zeros((NC, TILE, NB * F), jnp.float32)

    def propagate(blocks, copies, weight, dtype, wide, tiles=None):
        column = lax.all_to_all(copies, "blk", 0, 0, axis_index_groups=groups_along_z(), tiled=True)
        blocks, column = lax.optimization_barrier((blocks, column))
        near = [step(column, 1, True), step(column, -1, True)]
        opposite = step(column, 2, True)
        fetched = [from_behind(blocks, 2), swap_cores(blocks), swap_across(blocks), from_behind(blocks, -2)]
        first, last = jnp.stack([column, near[0]]), jnp.stack([near[1], opposite])
        if tiles is None:
            tiles = collect(me, dense_tiles, lax.optimization_barrier((first, other_tiles))[1])
        behind_first, ahead_last = step(first, 1, False), step(last, -1, False)
        behind_last, ahead_first = step(last, 1, False), step(first, -1, False)
        far = (step(behind_first, 1, False), step(ahead_last, -1, False))
        total = dense_part(me, 0, rows, (first, last), tiles, zeros)
        sparse = sparse_sums(me, sparse_row, sparse_src, sparse_count, fetch_list, blocks, fetched, sparse_tiles)
        total = dense_part(me, SIDE - 1, rows, (behind_first, behind_last), tiles, total)
        total = dense_part(me, 1, rows, (ahead_first, ahead_last), tiles, total)
        far, total, sparse = lax.optimization_barrier((far, total, sparse))
        total = dense_part(me, 2, rows, far, tiles, total)
        returned = swap_cores(total[1])
        return *finish(me, hub_block, total, returned, sparse, weight, dtype, wide), tiles

    blocks, copies = enter(me, hub_block, features)
    hidden, copies, tiles = propagate(blocks, copies, weight_one, jnp.bfloat16, True)
    embedded, _ = propagate(hidden, copies, weight_two, jnp.float32, False, tiles)
    return embedded.reshape(NB * TILE, F)


def solution(mesh):
    placed = (
        P("blk", None),
        P(),
        P(),
        P("blk", None, None),
        P("blk"),
        P(),
        P("blk", None, None),
        P("blk"),
        P("blk"),
        P("blk"),
        P("blk", None),
    )
    return jax.shard_map(shards, mesh=mesh, in_specs=placed, out_specs=P("blk", None), check_vma=False)
```

```python
import functools

import jax
import jax.numpy as jnp
from jax import lax
from jax.experimental import pallas as pl
from jax.experimental.pallas import tpu as pltpu
from jax.sharding import PartitionSpec as P


F = 128
TILE = 128
NB = 2
KS = 112
HOPS = 2
FETCH = 1
SOURCES = NB + 2 * HOPS * FETCH
NZ, NX, NY, NC = 8, 4, 4, 2
SHARDS = NZ * NX * NY * NC
SIDE = 4
TURNS = (0, SIDE - 1, 1, 2)

SMEM = pl.BlockSpec(memory_space=pltpu.SMEM)
VMEM = pl.BlockSpec(memory_space=pltpu.VMEM)
HBM = pl.BlockSpec(memory_space=pltpu.HBM)


def place(index):
    return index // (NX * NY * NC), index // (NY * NC) % NX, index // NC % NY, index % NC


def index_of(z, x, y, core):
    return ((z % NZ * NX + x % NX) * NY + y % NY) * NC + core % NC


def groups_along_z():
    return [[index_of(z, x, y, core) for z in range(NZ)] for x in range(NX) for y in range(NY) for core in range(NC)]


def step(array, by, across):
    pairs = []
    for index in range(SHARDS):
        z, x, y, core = place(index)
        along_x = (core == 0) != across
        pairs.append((index, index_of(z, x + (by if along_x else 0), y + (0 if along_x else by), core)))
    return lax.ppermute(array, "blk", pairs)


def swap_cores(array):
    return lax.ppermute(array, "blk", [(i, i ^ 1) for i in range(SHARDS)])


def from_behind(array, by):
    return lax.ppermute(array, "blk", [(i, (i + by) % SHARDS) for i in range(SHARDS)])


def placed_pair(block, row):
    zeros = jnp.zeros_like(block)
    return jnp.concatenate([jnp.where(row == 0, block, zeros), jnp.where(row == 0, zeros, block)], axis=1)


def enter_kernel(me_ref, hub_ref, features_ref, blocks_ref, copies_ref):
    blocks = [features_ref[b * TILE : (b + 1) * TILE].astype(jnp.bfloat16) for b in range(NB)]
    hub = jnp.where(hub_ref[me_ref[0]] == 0, blocks[0], blocks[1])
    for b in range(NB):
        blocks_ref[b] = blocks[b]
    for z in range(NZ):
        copies_ref[z] = hub


def enter(me, hub_block, features):
    return pl.pallas_call(
        enter_kernel,
        out_shape=(
            jax.ShapeDtypeStruct((NB, TILE, F), jnp.bfloat16),
            jax.ShapeDtypeStruct((NZ, TILE, F), jnp.bfloat16),
        ),
        in_specs=[SMEM, SMEM, VMEM],
        out_specs=(VMEM, VMEM),
        compiler_params=pltpu.CompilerParams(vmem_limit_bytes=8 << 20),
        name="enter",
    )(me, hub_block, features)


def sparse_kernel(me_ref, row_ref, src_ref, count_ref, fetch_ref, blocks_ref, beside_ref, behind_ref, ahead_ref, tiles_ref, out_ref, placed_ref):
    zeros = jnp.zeros((TILE, F), jnp.bfloat16)
    even = me_ref[0] % 2 == 0
    before, after = fetch_ref[0, 1], fetch_ref[0, 2]
    blocks = [
        blocks_ref[0],
        blocks_ref[1],
        behind_ref[0, fetch_ref[0, 0]],
        jnp.where(even, behind_ref[1, before], beside_ref[before]),
        jnp.where(even, beside_ref[after], ahead_ref[1, after]),
        ahead_ref[0, fetch_ref[0, 3]],
    ]
    for source in range(SOURCES):
        placed_ref[2 * source] = jnp.concatenate([blocks[source], zeros], axis=1)
        placed_ref[2 * source + 1] = jnp.concatenate([zeros, blocks[source]], axis=1)
    placed_ref[2 * SOURCES] = jnp.zeros((TILE, NB * F), jnp.bfloat16)
    out_ref[...] = jnp.zeros_like(out_ref)
    live = count_ref[0]

    def which(slot):
        return jnp.where(slot < live, 2 * src_ref[slot] + row_ref[slot], 2 * SOURCES)

    group = 8

    def add(at, _):
        first = at * group
        left = jnp.concatenate([tiles_ref[first + k] for k in range(group)], axis=1)
        right = jnp.concatenate([placed_ref[which(first + k)] for k in range(group)], axis=0)
        out_ref[...] += jnp.dot(left, right, preferred_element_type=jnp.float32)
        return 0

    lax.fori_loop(0, (live + group - 1) // group, add, 0)


def sparse_sums(me, row, src, count, wanted, near_blocks, tiles):
    return pl.pallas_call(
        sparse_kernel,
        out_shape=jax.ShapeDtypeStruct((TILE, NB * F), jnp.float32),
        in_specs=[SMEM] * 5 + [VMEM] * 5,
        out_specs=VMEM,
        scratch_shapes=[pltpu.VMEM((2 * SOURCES + 1, TILE, NB * F), jnp.bfloat16)],
        cost_estimate=pl.CostEstimate(flops=2 * KS * TILE**3, bytes_accessed=2 * KS * TILE**2, transcendentals=0),
        compiler_params=pltpu.CompilerParams(vmem_limit_bytes=16 << 20),
        name="sparse_sums",
    )(me, row, src, count, wanted, *near_blocks, tiles)


def collect_kernel(me_ref, own_ref, other_ref, out_ref, sems):
    core = me_ref[0] % NC
    copies = [
        pltpu.make_async_copy(tiles_ref.at[z, :, :, core], out_ref.at[side, z], sems.at[side, z])
        for side, tiles_ref in enumerate((own_ref, other_ref))
        for z in range(NZ)
    ]
    for copy in copies:
        copy.start()
    for copy in copies:
        copy.wait()


def collect(me, own, other):
    shape = (NZ, NX, NY, NC, TILE, TILE)
    return pl.pallas_call(
        collect_kernel,
        out_shape=jax.ShapeDtypeStruct((NC, NZ, NX, NY, TILE, TILE), jnp.bfloat16),
        in_specs=[SMEM, HBM, HBM],
        out_specs=VMEM,
        scratch_shapes=[pltpu.SemaphoreType.DMA((NC, NZ))],
        compiler_params=pltpu.CompilerParams(vmem_limit_bytes=44 << 20),
        cost_estimate=pl.CostEstimate(flops=0, bytes_accessed=2 * SHARDS * TILE**2, transcendentals=0),
        name="collect",
    )(me, own.reshape(shape), other.reshape(shape))


def dense_kernel(halves, me_ref, shift_ref, own_row_ref, other_row_ref, *refs):
    chunk_refs, (tiles_ref, start_ref, out_ref) = refs[:halves], refs[halves:]
    me = me_ref[0]
    x, y, core = me // (NY * NC) % NX, me // NC % NY, me % NC
    fixed = (jnp.where(core == 0, x, y) + shift_ref[0]) % SIDE
    out_ref[...] = start_ref[...]
    for k, turn in enumerate(TURNS):
        chunk_ref, at = chunk_refs[k * halves // SIDE], k % (SIDE // halves)
        along = (jnp.where(core == 0, y, x) + turn) % SIDE
        at_x = jnp.where(core == 0, fixed, along)
        at_y = jnp.where(core == 0, along, fixed)
        sources = [((z * NX + at_x) * NY + at_y) * NC + core for z in range(NZ)]
        for side, row_ref in enumerate((own_row_ref, other_row_ref)):
            left = jnp.concatenate([tiles_ref[side, z, at_x, at_y] for z in range(NZ)], axis=1)
            right = jnp.concatenate(
                [placed_pair(chunk_ref[at, z], row_ref[source]) for z, source in enumerate(sources)], axis=0
            )
            out_ref[side] += jnp.dot(left, right, preferred_element_type=jnp.float32)


def dense_part(me, shift, rows, chunks, tiles, start):
    return pl.pallas_call(
        functools.partial(dense_kernel, len(chunks)),
        out_shape=jax.ShapeDtypeStruct((NC, TILE, NB * F), jnp.float32),
        in_specs=[SMEM] * 4 + [VMEM] * (len(chunks) + 2),
        out_specs=VMEM,
        compiler_params=pltpu.CompilerParams(vmem_limit_bytes=16 << 20),
        cost_estimate=pl.CostEstimate(
            flops=8 * SIDE * NZ * TILE**3, bytes_accessed=6 * SIDE * NZ * TILE**2, transcendentals=0
        ),
        name="dense_part",
    )(me, jnp.array([shift], jnp.int32), *rows, *chunks, tiles, start)


def finish_kernel(wide, me_ref, hub_ref, dense_ref, other_ref, sparse_ref, weight_ref, out_ref, *copies):
    blocks = []
    for block in range(NB):
        columns = slice(block * F, (block + 1) * F)
        summed = dense_ref[0, :, columns] + other_ref[:, columns] + sparse_ref[:, columns]
        projected = jnp.dot(
            summed, weight_ref[...], precision=lax.Precision.HIGHEST, preferred_element_type=jnp.float32
        )
        blocks.append(jnp.maximum(projected, 0.0).astype(out_ref.dtype))
        out_ref[block] = blocks[block]
    if wide:
        hub = jnp.where(hub_ref[me_ref[0]] == 0, blocks[0], blocks[1])
        for z in range(NZ):
            copies[0][z] = hub


def finish(me, hub_block, dense, other, sparse, weight, dtype, wide):
    shape = jax.ShapeDtypeStruct((NB, TILE, F), dtype)
    copies = [jax.ShapeDtypeStruct((NZ, TILE, F), dtype)] if wide else []
    return pl.pallas_call(
        functools.partial(finish_kernel, wide),
        out_shape=(shape, *copies),
        in_specs=[SMEM, SMEM] + [VMEM] * 4,
        out_specs=(VMEM,) * (1 + len(copies)),
        compiler_params=pltpu.CompilerParams(vmem_limit_bytes=8 << 20),
        name="finish",
    )(me, hub_block, dense, other, sparse, weight)


def shards(
    features,
    weight_one,
    weight_two,
    dense_tiles,
    dense_row,
    hub_block,
    sparse_tiles,
    sparse_row,
    sparse_src,
    sparse_count,
    fetch_list,
):
    me = lax.axis_index("blk").astype(jnp.int32).reshape(1)
    rows = [dense_row, swap_cores(dense_row)]
    other_tiles = swap_cores(dense_tiles)
    zeros = jnp.zeros((NC, TILE, NB * F), jnp.float32)

    def propagate(blocks, copies, weight, dtype, wide, tiles=None):
        column = lax.all_to_all(copies, "blk", 0, 0, axis_index_groups=groups_along_z(), tiled=True)
        beside = swap_cores(blocks)
        pair = jnp.stack([blocks, beside])
        fetched = [from_behind(pair, NC), from_behind(pair, -NC)]
        column, fetched = lax.optimization_barrier((column, fetched))
        near = [step(column, 1, True), step(column, -1, True)]
        opposite = step(column, 2, True)
        first, last = jnp.stack([column, near[0]]), jnp.stack([near[1], opposite])
        if tiles is None:
            tiles = collect(me, dense_tiles, lax.optimization_barrier((first, other_tiles))[1])
        behind_first, ahead_last = step(first, 1, False), step(last, -1, False)
        behind_last, ahead_first = step(last, 1, False), step(first, -1, False)
        far = (step(behind_first, 1, False), step(ahead_last, -1, False))
        total = dense_part(me, 0, rows, (first, last), tiles, zeros)
        near_blocks, total = lax.optimization_barrier(((blocks, beside, *fetched), total))
        sparse = sparse_sums(me, sparse_row, sparse_src, sparse_count, fetch_list, near_blocks, sparse_tiles)
        total = dense_part(me, SIDE - 1, rows, (behind_first, behind_last), tiles, total)
        total = dense_part(me, 1, rows, (ahead_first, ahead_last), tiles, total)
        far, total, sparse = lax.optimization_barrier((far, total, sparse))
        total = dense_part(me, 2, rows, far, tiles, total)
        returned = swap_cores(total[1])
        return *finish(me, hub_block, total, returned, sparse, weight, dtype, wide), tiles

    blocks, copies = enter(me, hub_block, features)
    hidden, copies, tiles = propagate(blocks, copies, weight_one, jnp.bfloat16, True)
    embedded, _ = propagate(hidden, copies, weight_two, jnp.float32, False, tiles)
    return embedded.reshape(NB * TILE, F)


def solution(mesh):
    placed = (
        P("blk", None),
        P(),
        P(),
        P("blk", None, None),
        P("blk"),
        P(),
        P("blk", None, None),
        P("blk"),
        P("blk"),
        P("blk"),
        P("blk", None),
    )
    return jax.shard_map(shards, mesh=mesh, in_specs=placed, out_specs=P("blk", None), check_vma=False)
```

```python
import functools

import jax
import jax.numpy as jnp
from jax import lax
from jax.experimental import pallas as pl
from jax.experimental.pallas import tpu as pltpu
from jax.sharding import PartitionSpec as P


F = 128
TILE = 128
NB = 2
KS = 112
HOPS = 2
FETCH = 1
SOURCES = NB + 2 * HOPS * FETCH
NZ, NX, NY, NC = 8, 4, 4, 2
SHARDS = NZ * NX * NY * NC
SIDE = 4
TURNS = (0, SIDE - 1, 1, 2)

SMEM = pl.BlockSpec(memory_space=pltpu.SMEM)
VMEM = pl.BlockSpec(memory_space=pltpu.VMEM)
HBM = pl.BlockSpec(memory_space=pltpu.HBM)


def place(index):
    return index // (NX * NY * NC), index // (NY * NC) % NX, index // NC % NY, index % NC


def index_of(z, x, y, core):
    return ((z % NZ * NX + x % NX) * NY + y % NY) * NC + core % NC


def groups_along_z():
    return [[index_of(z, x, y, core) for z in range(NZ)] for x in range(NX) for y in range(NY) for core in range(NC)]


def step(array, by, across):
    pairs = []
    for index in range(SHARDS):
        z, x, y, core = place(index)
        along_x = (core == 0) != across
        pairs.append((index, index_of(z, x + (by if along_x else 0), y + (0 if along_x else by), core)))
    return lax.ppermute(array, "blk", pairs)


def swap_cores(array):
    return lax.ppermute(array, "blk", [(i, i ^ 1) for i in range(SHARDS)])


def from_chips(array):
    return lax.ppermute(array, "blk", [(i, (i + (-NC if i % NC else NC)) % SHARDS) for i in range(SHARDS)])


def placed_pair(block, row):
    zeros = jnp.zeros_like(block)
    return jnp.concatenate([jnp.where(row == 0, block, zeros), jnp.where(row == 0, zeros, block)], axis=1)


def enter_kernel(me_ref, hub_ref, features_ref, blocks_ref, copies_ref):
    blocks = [features_ref[b * TILE : (b + 1) * TILE].astype(jnp.bfloat16) for b in range(NB)]
    hub = jnp.where(hub_ref[me_ref[0]] == 0, blocks[0], blocks[1])
    for b in range(NB):
        blocks_ref[b] = blocks[b]
    for z in range(NZ):
        copies_ref[z] = hub


def enter(me, hub_block, features):
    return pl.pallas_call(
        enter_kernel,
        out_shape=(
            jax.ShapeDtypeStruct((NB, TILE, F), jnp.bfloat16),
            jax.ShapeDtypeStruct((NZ, TILE, F), jnp.bfloat16),
        ),
        in_specs=[SMEM, SMEM, VMEM],
        out_specs=(VMEM, VMEM),
        compiler_params=pltpu.CompilerParams(vmem_limit_bytes=8 << 20),
        name="enter",
    )(me, hub_block, features)


def sparse_kernel(me_ref, row_ref, src_ref, count_ref, fetch_ref, blocks_ref, beside_ref, fetched_ref, shared_ref, tiles_ref, out_ref, placed_ref):
    zeros = jnp.zeros((TILE, F), jnp.bfloat16)
    even = me_ref[0] % NC == 0
    wanted = [fetch_ref[0, entry] for entry in range(2 * HOPS)]
    blocks = [
        blocks_ref[0],
        blocks_ref[1],
        jnp.where(even, fetched_ref[0, wanted[0]], shared_ref[1, wanted[0]]),
        jnp.where(even, fetched_ref[1, wanted[1]], beside_ref[wanted[1]]),
        jnp.where(even, beside_ref[wanted[2]], fetched_ref[1, wanted[2]]),
        jnp.where(even, shared_ref[1, wanted[3]], fetched_ref[0, wanted[3]]),
    ]
    for source in range(SOURCES):
        placed_ref[2 * source] = jnp.concatenate([blocks[source], zeros], axis=1)
        placed_ref[2 * source + 1] = jnp.concatenate([zeros, blocks[source]], axis=1)
    placed_ref[2 * SOURCES] = jnp.zeros((TILE, NB * F), jnp.bfloat16)
    out_ref[...] = jnp.zeros_like(out_ref)
    live = count_ref[0]

    def which(slot):
        return jnp.where(slot < live, 2 * src_ref[slot] + row_ref[slot], 2 * SOURCES)

    group = 8

    def add(at, _):
        first = at * group
        left = jnp.concatenate([tiles_ref[first + k] for k in range(group)], axis=1)
        right = jnp.concatenate([placed_ref[which(first + k)] for k in range(group)], axis=0)
        out_ref[...] += jnp.dot(left, right, preferred_element_type=jnp.float32)
        return 0

    lax.fori_loop(0, (live + group - 1) // group, add, 0)


def sparse_sums(me, row, src, count, wanted, near_blocks, tiles):
    return pl.pallas_call(
        sparse_kernel,
        out_shape=jax.ShapeDtypeStruct((TILE, NB * F), jnp.float32),
        in_specs=[SMEM] * 5 + [VMEM] * 5,
        out_specs=VMEM,
        scratch_shapes=[pltpu.VMEM((2 * SOURCES + 1, TILE, NB * F), jnp.bfloat16)],
        cost_estimate=pl.CostEstimate(flops=2 * KS * TILE**3, bytes_accessed=2 * KS * TILE**2, transcendentals=0),
        compiler_params=pltpu.CompilerParams(vmem_limit_bytes=16 << 20),
        name="sparse_sums",
    )(me, row, src, count, wanted, *near_blocks, tiles)


def collect_kernel(me_ref, own_ref, other_ref, out_ref, sems):
    core = me_ref[0] % NC
    copies = [
        pltpu.make_async_copy(tiles_ref.at[z, :, :, core], out_ref.at[side, z], sems.at[side, z])
        for side, tiles_ref in enumerate((own_ref, other_ref))
        for z in range(NZ)
    ]
    for copy in copies:
        copy.start()
    for copy in copies:
        copy.wait()


def collect(me, own, other):
    shape = (NZ, NX, NY, NC, TILE, TILE)
    return pl.pallas_call(
        collect_kernel,
        out_shape=jax.ShapeDtypeStruct((NC, NZ, NX, NY, TILE, TILE), jnp.bfloat16),
        in_specs=[SMEM, HBM, HBM],
        out_specs=VMEM,
        scratch_shapes=[pltpu.SemaphoreType.DMA((NC, NZ))],
        compiler_params=pltpu.CompilerParams(vmem_limit_bytes=44 << 20),
        cost_estimate=pl.CostEstimate(flops=0, bytes_accessed=2 * SHARDS * TILE**2, transcendentals=0),
        name="collect",
    )(me, own.reshape(shape), other.reshape(shape))


def dense_kernel(halves, me_ref, shift_ref, own_row_ref, other_row_ref, *refs):
    chunk_refs, (tiles_ref, start_ref, out_ref) = refs[:halves], refs[halves:]
    me = me_ref[0]
    x, y, core = me // (NY * NC) % NX, me // NC % NY, me % NC
    fixed = (jnp.where(core == 0, x, y) + shift_ref[0]) % SIDE
    out_ref[...] = start_ref[...]
    for k, turn in enumerate(TURNS):
        chunk_ref, at = chunk_refs[k * halves // SIDE], k % (SIDE // halves)
        along = (jnp.where(core == 0, y, x) + turn) % SIDE
        at_x = jnp.where(core == 0, fixed, along)
        at_y = jnp.where(core == 0, along, fixed)
        sources = [((z * NX + at_x) * NY + at_y) * NC + core for z in range(NZ)]
        for side, row_ref in enumerate((own_row_ref, other_row_ref)):
            left = jnp.concatenate([tiles_ref[side, z, at_x, at_y] for z in range(NZ)], axis=1)
            right = jnp.concatenate(
                [placed_pair(chunk_ref[at, z], row_ref[source]) for z, source in enumerate(sources)], axis=0
            )
            out_ref[side] += jnp.dot(left, right, preferred_element_type=jnp.float32)


def dense_part(me, shift, rows, chunks, tiles, start):
    return pl.pallas_call(
        functools.partial(dense_kernel, len(chunks)),
        out_shape=jax.ShapeDtypeStruct((NC, TILE, NB * F), jnp.float32),
        in_specs=[SMEM] * 4 + [VMEM] * (len(chunks) + 2),
        out_specs=VMEM,
        compiler_params=pltpu.CompilerParams(vmem_limit_bytes=16 << 20),
        cost_estimate=pl.CostEstimate(
            flops=8 * SIDE * NZ * TILE**3, bytes_accessed=6 * SIDE * NZ * TILE**2, transcendentals=0
        ),
        name="dense_part",
    )(me, jnp.array([shift], jnp.int32), *rows, *chunks, tiles, start)


def finish_kernel(wide, me_ref, hub_ref, dense_ref, other_ref, sparse_ref, weight_ref, out_ref, *copies):
    blocks = []
    for block in range(NB):
        columns = slice(block * F, (block + 1) * F)
        summed = dense_ref[0, :, columns] + other_ref[:, columns] + sparse_ref[:, columns]
        projected = jnp.dot(
            summed, weight_ref[...], precision=lax.Precision.HIGHEST, preferred_element_type=jnp.float32
        )
        blocks.append(jnp.maximum(projected, 0.0).astype(out_ref.dtype))
        out_ref[block] = blocks[block]
    if wide:
        hub = jnp.where(hub_ref[me_ref[0]] == 0, blocks[0], blocks[1])
        for z in range(NZ):
            copies[0][z] = hub


def finish(me, hub_block, dense, other, sparse, weight, dtype, wide):
    shape = jax.ShapeDtypeStruct((NB, TILE, F), dtype)
    copies = [jax.ShapeDtypeStruct((NZ, TILE, F), dtype)] if wide else []
    return pl.pallas_call(
        functools.partial(finish_kernel, wide),
        out_shape=(shape, *copies),
        in_specs=[SMEM, SMEM] + [VMEM] * 4,
        out_specs=(VMEM,) * (1 + len(copies)),
        compiler_params=pltpu.CompilerParams(vmem_limit_bytes=8 << 20),
        name="finish",
    )(me, hub_block, dense, other, sparse, weight)


def shards(
    features,
    weight_one,
    weight_two,
    dense_tiles,
    dense_row,
    hub_block,
    sparse_tiles,
    sparse_row,
    sparse_src,
    sparse_count,
    fetch_list,
):
    me = lax.axis_index("blk").astype(jnp.int32).reshape(1)
    rows = [dense_row, swap_cores(dense_row)]
    other_tiles = swap_cores(dense_tiles)
    zeros = jnp.zeros((NC, TILE, NB * F), jnp.float32)

    def propagate(blocks, copies, weight, dtype, wide, tiles=None):
        column = lax.all_to_all(copies, "blk", 0, 0, axis_index_groups=groups_along_z(), tiled=True)
        blocks, column = lax.optimization_barrier((blocks, column))
        beside = swap_cores(blocks)
        pair = jnp.stack([blocks, beside])
        side_behind = step(column, 1, True)
        side_ahead = step(column, -1, True)
        opposite = step(column, 2, True)
        fetched = from_chips(pair)
        first, last = jnp.stack([column, side_behind]), jnp.stack([side_ahead, opposite])
        if tiles is None:
            tiles = collect(me, dense_tiles, lax.optimization_barrier((first, other_tiles))[1])
        behind_first = step(first, 1, False)
        ahead_last = step(last, -1, False)
        behind_last, ahead_first = step(last, 1, False), step(first, -1, False)
        shared = swap_cores(fetched)
        far = (step(behind_first, 1, False), step(ahead_last, -1, False))
        total = dense_part(me, 0, rows, (first, last), tiles, zeros)
        near_blocks, total = lax.optimization_barrier(((blocks, beside, fetched, shared), total))
        sparse = sparse_sums(me, sparse_row, sparse_src, sparse_count, fetch_list, near_blocks, sparse_tiles)
        total = dense_part(me, SIDE - 1, rows, (behind_first, behind_last), tiles, total)
        total = dense_part(me, 1, rows, (ahead_first, ahead_last), tiles, total)
        far, total, sparse = lax.optimization_barrier((far, total, sparse))
        total = dense_part(me, 2, rows, far, tiles, total)
        returned = swap_cores(total[1])
        return *finish(me, hub_block, total, returned, sparse, weight, dtype, wide), tiles

    blocks, copies = enter(me, hub_block, features)
    hidden, copies, tiles = propagate(blocks, copies, weight_one, jnp.bfloat16, True)
    embedded, _ = propagate(hidden, copies, weight_two, jnp.float32, False, tiles)
    return embedded.reshape(NB * TILE, F)


def solution(mesh):
    placed = (
        P("blk", None),
        P(),
        P(),
        P("blk", None, None),
        P("blk"),
        P(),
        P("blk", None, None),
        P("blk"),
        P("blk"),
        P("blk"),
        P("blk", None),
    )
    return jax.shard_map(shards, mesh=mesh, in_specs=placed, out_specs=P("blk", None), check_vma=False)
```

```python
import functools

import jax
import jax.numpy as jnp
from jax import lax
from jax.experimental import pallas as pl
from jax.experimental.pallas import tpu as pltpu
from jax.sharding import PartitionSpec as P


F = 128
TILE = 128
NB = 2
KS = 112
HOPS = 2
FETCH = 1
SOURCES = NB + 2 * HOPS * FETCH
NZ, NX, NY, NC = 8, 4, 4, 2
SHARDS = NZ * NX * NY * NC
SIDE = 4
TURNS = (0, SIDE - 1, 1, 2)

SMEM = pl.BlockSpec(memory_space=pltpu.SMEM)
VMEM = pl.BlockSpec(memory_space=pltpu.VMEM)
HBM = pl.BlockSpec(memory_space=pltpu.HBM)


def place(index):
    return index // (NX * NY * NC), index // (NY * NC) % NX, index // NC % NY, index % NC


def index_of(z, x, y, core):
    return ((z % NZ * NX + x % NX) * NY + y % NY) * NC + core % NC


def groups_along_z():
    return [[index_of(z, x, y, core) for z in range(NZ)] for x in range(NX) for y in range(NY) for core in range(NC)]


def step(array, by, across):
    pairs = []
    for index in range(SHARDS):
        z, x, y, core = place(index)
        along_x = (core == 0) != across
        pairs.append((index, index_of(z, x + (by if along_x else 0), y + (0 if along_x else by), core)))
    return lax.ppermute(array, "blk", pairs)


def swap_cores(array):
    return lax.ppermute(array, "blk", [(i, i ^ 1) for i in range(SHARDS)])


def from_chips(array):
    return lax.ppermute(array, "blk", [(i, (i + (-NC if i % NC else NC)) % SHARDS) for i in range(SHARDS)])


def placed_pair(block, row):
    zeros = jnp.zeros_like(block)
    return jnp.concatenate([jnp.where(row == 0, block, zeros), jnp.where(row == 0, zeros, block)], axis=1)


def enter_kernel(me_ref, hub_ref, features_ref, blocks_ref, copies_ref):
    blocks = [features_ref[b * TILE : (b + 1) * TILE].astype(jnp.bfloat16) for b in range(NB)]
    hub = jnp.where(hub_ref[me_ref[0]] == 0, blocks[0], blocks[1])
    for b in range(NB):
        blocks_ref[b] = blocks[b]
    for z in range(NZ):
        copies_ref[z] = hub


def enter(me, hub_block, features):
    return pl.pallas_call(
        enter_kernel,
        out_shape=(
            jax.ShapeDtypeStruct((NB, TILE, F), jnp.bfloat16),
            jax.ShapeDtypeStruct((NZ, TILE, F), jnp.bfloat16),
        ),
        in_specs=[SMEM, SMEM, VMEM],
        out_specs=(VMEM, VMEM),
        compiler_params=pltpu.CompilerParams(vmem_limit_bytes=8 << 20),
        name="enter",
    )(me, hub_block, features)


def sparse_kernel(me_ref, row_ref, src_ref, count_ref, fetch_ref, blocks_ref, beside_ref, fetched_ref, shared_ref, tiles_ref, out_ref, placed_ref):
    zeros = jnp.zeros((TILE, F), jnp.bfloat16)
    even = me_ref[0] % NC == 0
    wanted = [fetch_ref[0, entry] for entry in range(2 * HOPS)]
    blocks = [
        blocks_ref[0],
        blocks_ref[1],
        jnp.where(even, fetched_ref[0, wanted[0]], shared_ref[1, wanted[0]]),
        jnp.where(even, fetched_ref[1, wanted[1]], beside_ref[wanted[1]]),
        jnp.where(even, beside_ref[wanted[2]], fetched_ref[1, wanted[2]]),
        jnp.where(even, shared_ref[1, wanted[3]], fetched_ref[0, wanted[3]]),
    ]
    for source in range(SOURCES):
        placed_ref[2 * source] = jnp.concatenate([blocks[source], zeros], axis=1)
        placed_ref[2 * source + 1] = jnp.concatenate([zeros, blocks[source]], axis=1)
    placed_ref[2 * SOURCES] = jnp.zeros((TILE, NB * F), jnp.bfloat16)
    out_ref[...] = jnp.zeros_like(out_ref)
    live = count_ref[0]

    def which(slot):
        return jnp.where(slot < live, 2 * src_ref[slot] + row_ref[slot], 2 * SOURCES)

    group = 8

    def add(at, _):
        first = at * group
        left = jnp.concatenate([tiles_ref[first + k] for k in range(group)], axis=1)
        right = jnp.concatenate([placed_ref[which(first + k)] for k in range(group)], axis=0)
        out_ref[...] += jnp.dot(left, right, preferred_element_type=jnp.float32)
        return 0

    lax.fori_loop(0, (live + group - 1) // group, add, 0)


def sparse_sums(me, row, src, count, wanted, near_blocks, tiles):
    return pl.pallas_call(
        sparse_kernel,
        out_shape=jax.ShapeDtypeStruct((TILE, NB * F), jnp.float32),
        in_specs=[SMEM] * 5 + [VMEM] * 5,
        out_specs=VMEM,
        scratch_shapes=[pltpu.VMEM((2 * SOURCES + 1, TILE, NB * F), jnp.bfloat16)],
        cost_estimate=pl.CostEstimate(flops=2 * KS * TILE**3, bytes_accessed=2 * KS * TILE**2, transcendentals=0),
        compiler_params=pltpu.CompilerParams(vmem_limit_bytes=16 << 20),
        name="sparse_sums",
    )(me, row, src, count, wanted, *near_blocks, tiles)


def collect_kernel(me_ref, own_ref, other_ref, out_ref, sems):
    core = me_ref[0] % NC
    copies = [
        pltpu.make_async_copy(tiles_ref.at[z, :, :, core], out_ref.at[side, z], sems.at[side, z])
        for side, tiles_ref in enumerate((own_ref, other_ref))
        for z in range(NZ)
    ]
    for copy in copies:
        copy.start()
    for copy in copies:
        copy.wait()


def collect(me, own, other):
    shape = (NZ, NX, NY, NC, TILE, TILE)
    return pl.pallas_call(
        collect_kernel,
        out_shape=jax.ShapeDtypeStruct((NC, NZ, NX, NY, TILE, TILE), jnp.bfloat16),
        in_specs=[SMEM, HBM, HBM],
        out_specs=VMEM,
        scratch_shapes=[pltpu.SemaphoreType.DMA((NC, NZ))],
        compiler_params=pltpu.CompilerParams(vmem_limit_bytes=44 << 20),
        cost_estimate=pl.CostEstimate(flops=0, bytes_accessed=2 * SHARDS * TILE**2, transcendentals=0),
        name="collect",
    )(me, own.reshape(shape), other.reshape(shape))


def dense_kernel(halves, turns, me_ref, shift_ref, own_row_ref, other_row_ref, *refs):
    chunk_refs, (tiles_ref, start_ref, out_ref) = refs[:halves], refs[halves:]
    me = me_ref[0]
    x, y, core = me // (NY * NC) % NX, me // NC % NY, me % NC
    fixed = (jnp.where(core == 0, x, y) + shift_ref[0]) % SIDE
    out_ref[...] = start_ref[...]
    for k, turn in enumerate(turns):
        chunk_ref, at = chunk_refs[k * halves // len(turns)], k % (len(turns) // halves)
        along = (jnp.where(core == 0, y, x) + turn) % SIDE
        at_x = jnp.where(core == 0, fixed, along)
        at_y = jnp.where(core == 0, along, fixed)
        sources = [((z * NX + at_x) * NY + at_y) * NC + core for z in range(NZ)]
        for side, row_ref in enumerate((own_row_ref, other_row_ref)):
            left = jnp.concatenate([tiles_ref[side, z, at_x, at_y] for z in range(NZ)], axis=1)
            right = jnp.concatenate(
                [placed_pair(chunk_ref[at, z], row_ref[source]) for z, source in enumerate(sources)], axis=0
            )
            out_ref[side] += jnp.dot(left, right, preferred_element_type=jnp.float32)


def dense_part(me, shift, rows, chunks, tiles, start, turns=TURNS):
    return pl.pallas_call(
        functools.partial(dense_kernel, len(chunks), turns),
        out_shape=jax.ShapeDtypeStruct((NC, TILE, NB * F), jnp.float32),
        in_specs=[SMEM] * 4 + [VMEM] * (len(chunks) + 2),
        out_specs=VMEM,
        compiler_params=pltpu.CompilerParams(vmem_limit_bytes=16 << 20),
        cost_estimate=pl.CostEstimate(
            flops=4 * NC * len(turns) * NZ * TILE**3,
            bytes_accessed=6 * len(turns) * NZ * TILE**2,
            transcendentals=0,
        ),
        name="dense_part",
    )(me, jnp.array([shift], jnp.int32), *rows, *chunks, tiles, start)


def finish_kernel(wide, me_ref, hub_ref, dense_ref, other_ref, sparse_ref, weight_ref, out_ref, *copies):
    blocks = []
    for block in range(NB):
        columns = slice(block * F, (block + 1) * F)
        summed = dense_ref[0, :, columns] + other_ref[:, columns] + sparse_ref[:, columns]
        projected = jnp.dot(
            summed, weight_ref[...], precision=lax.Precision.HIGHEST, preferred_element_type=jnp.float32
        )
        blocks.append(jnp.maximum(projected, 0.0).astype(out_ref.dtype))
        out_ref[block] = blocks[block]
    if wide:
        hub = jnp.where(hub_ref[me_ref[0]] == 0, blocks[0], blocks[1])
        for z in range(NZ):
            copies[0][z] = hub


def finish(me, hub_block, dense, other, sparse, weight, dtype, wide):
    shape = jax.ShapeDtypeStruct((NB, TILE, F), dtype)
    copies = [jax.ShapeDtypeStruct((NZ, TILE, F), dtype)] if wide else []
    return pl.pallas_call(
        functools.partial(finish_kernel, wide),
        out_shape=(shape, *copies),
        in_specs=[SMEM, SMEM] + [VMEM] * 4,
        out_specs=(VMEM,) * (1 + len(copies)),
        compiler_params=pltpu.CompilerParams(vmem_limit_bytes=8 << 20),
        name="finish",
    )(me, hub_block, dense, other, sparse, weight)


def shards(
    features,
    weight_one,
    weight_two,
    dense_tiles,
    dense_row,
    hub_block,
    sparse_tiles,
    sparse_row,
    sparse_src,
    sparse_count,
    fetch_list,
):
    me = lax.axis_index("blk").astype(jnp.int32).reshape(1)
    rows = [dense_row, swap_cores(dense_row)]
    other_tiles = swap_cores(dense_tiles)
    zeros = jnp.zeros((NC, TILE, NB * F), jnp.float32)

    def propagate(blocks, copies, weight, dtype, wide, tiles=None):
        column = lax.all_to_all(copies, "blk", 0, 0, axis_index_groups=groups_along_z(), tiled=True)
        blocks, column = lax.optimization_barrier((blocks, column))
        beside = swap_cores(blocks)
        pair = jnp.stack([blocks, beside])
        side_behind = step(column, 1, True)
        side_ahead = step(column, -1, True)
        opposite = step(column, 2, True)
        fetched = from_chips(pair)
        first = jnp.stack([column, side_behind])
        last = jnp.stack([side_ahead, opposite])
        if tiles is None:
            tiles = collect(me, dense_tiles, lax.optimization_barrier((first, other_tiles))[1])
        behind_first = step(first, 1, False)
        ahead_last = step(last, -1, False)
        behind_last, ahead_first = step(last, 1, False), step(first, -1, False)
        shared = swap_cores(fetched)
        far = (step(behind_first, 1, False), step(ahead_last, -1, False))
        total = dense_part(me, 0, rows, (first, last), tiles, zeros)
        near_blocks, total = lax.optimization_barrier(((blocks, beside, fetched, shared), total))
        sparse = sparse_sums(me, sparse_row, sparse_src, sparse_count, fetch_list, near_blocks, sparse_tiles)
        total = dense_part(me, SIDE - 1, rows, (behind_first, behind_last), tiles, total)
        total = dense_part(me, 1, rows, (ahead_first, ahead_last), tiles, total)
        far_first, total, sparse = lax.optimization_barrier((far[0], total, sparse))
        total = dense_part(me, 2, rows, (far_first,), tiles, total, TURNS[: SIDE // 2])
        total = dense_part(me, 2, rows, (far[1],), tiles, total, TURNS[SIDE // 2 :])
        returned = swap_cores(total[1])
        return *finish(me, hub_block, total, returned, sparse, weight, dtype, wide), tiles

    blocks, copies = enter(me, hub_block, features)
    hidden, copies, tiles = propagate(blocks, copies, weight_one, jnp.bfloat16, True)
    embedded, _ = propagate(hidden, copies, weight_two, jnp.float32, False, tiles)
    return embedded.reshape(NB * TILE, F)


def solution(mesh):
    placed = (
        P("blk", None),
        P(),
        P(),
        P("blk", None, None),
        P("blk"),
        P(),
        P("blk", None, None),
        P("blk"),
        P("blk"),
        P("blk"),
        P("blk", None),
    )
    return jax.shard_map(shards, mesh=mesh, in_specs=placed, out_specs=P("blk", None), check_vma=False)
```

```python
import functools

import jax
import jax.numpy as jnp
from jax import lax
from jax.experimental import pallas as pl
from jax.experimental.pallas import tpu as pltpu
from jax.sharding import PartitionSpec as P


F = 128
TILE = 128
NB = 2
KS = 112
HOPS = 2
FETCH = 1
SOURCES = NB + 2 * HOPS * FETCH
NZ, NX, NY, NC = 8, 4, 4, 2
SHARDS = NZ * NX * NY * NC
SIDE = 4
TURNS = (0, SIDE - 1, 1, 2)

SMEM = pl.BlockSpec(memory_space=pltpu.SMEM)
VMEM = pl.BlockSpec(memory_space=pltpu.VMEM)
HBM = pl.BlockSpec(memory_space=pltpu.HBM)


def place(index):
    return index // (NX * NY * NC), index // (NY * NC) % NX, index // NC % NY, index % NC


def index_of(z, x, y, core):
    return ((z % NZ * NX + x % NX) * NY + y % NY) * NC + core % NC


def groups_along_z():
    return [[index_of(z, x, y, core) for z in range(NZ)] for x in range(NX) for y in range(NY) for core in range(NC)]


def step(array, by, across):
    pairs = []
    for index in range(SHARDS):
        z, x, y, core = place(index)
        along_x = (core == 0) != across
        pairs.append((index, index_of(z, x + (by if along_x else 0), y + (0 if along_x else by), core)))
    return lax.ppermute(array, "blk", pairs)


def swap_cores(array):
    return lax.ppermute(array, "blk", [(i, i ^ 1) for i in range(SHARDS)])


def from_chips(array):
    return lax.ppermute(array, "blk", [(i, (i + (-NC if i % NC else NC)) % SHARDS) for i in range(SHARDS)])


def placed_pair(block, row):
    zeros = jnp.zeros_like(block)
    return jnp.concatenate([jnp.where(row == 0, block, zeros), jnp.where(row == 0, zeros, block)], axis=1)


def enter_kernel(hub_ref, features_ref, blocks_ref, copies_ref):
    blocks = [features_ref[b * TILE : (b + 1) * TILE].astype(jnp.bfloat16) for b in range(NB)]
    hub = jnp.where(hub_ref[lax.axis_index("blk")] == 0, blocks[0], blocks[1])
    for b in range(NB):
        blocks_ref[b] = blocks[b]
    for z in range(NZ):
        copies_ref[z] = hub


def enter(hub_block, features):
    return pl.pallas_call(
        enter_kernel,
        out_shape=(
            jax.ShapeDtypeStruct((NB, TILE, F), jnp.bfloat16),
            jax.ShapeDtypeStruct((NZ, TILE, F), jnp.bfloat16),
        ),
        in_specs=[SMEM, VMEM],
        out_specs=(VMEM, VMEM),
        compiler_params=pltpu.CompilerParams(vmem_limit_bytes=8 << 20),
        name="enter",
    )(hub_block, features)


def sparse_kernel(row_ref, src_ref, count_ref, fetch_ref, blocks_ref, beside_ref, fetched_ref, shared_ref, tiles_ref, out_ref, placed_ref):
    zeros = jnp.zeros((TILE, F), jnp.bfloat16)
    even = lax.axis_index("blk") % NC == 0
    wanted = [fetch_ref[0, entry] for entry in range(2 * HOPS)]
    blocks = [
        blocks_ref[0],
        blocks_ref[1],
        jnp.where(even, fetched_ref[0, wanted[0]], shared_ref[1, wanted[0]]),
        jnp.where(even, fetched_ref[1, wanted[1]], beside_ref[wanted[1]]),
        jnp.where(even, beside_ref[wanted[2]], fetched_ref[1, wanted[2]]),
        jnp.where(even, shared_ref[1, wanted[3]], fetched_ref[0, wanted[3]]),
    ]
    for source in range(SOURCES):
        placed_ref[2 * source] = jnp.concatenate([blocks[source], zeros], axis=1)
        placed_ref[2 * source + 1] = jnp.concatenate([zeros, blocks[source]], axis=1)
    placed_ref[2 * SOURCES] = jnp.zeros((TILE, NB * F), jnp.bfloat16)
    out_ref[...] = jnp.zeros_like(out_ref)
    live = count_ref[0]

    def which(slot):
        return jnp.where(slot < live, 2 * src_ref[slot] + row_ref[slot], 2 * SOURCES)

    group = 8

    def add(at, _):
        first = at * group
        left = jnp.concatenate([tiles_ref[first + k] for k in range(group)], axis=1)
        right = jnp.concatenate([placed_ref[which(first + k)] for k in range(group)], axis=0)
        out_ref[...] += jnp.dot(left, right, preferred_element_type=jnp.float32)
        return 0

    lax.fori_loop(0, (live + group - 1) // group, add, 0)


def sparse_sums(row, src, count, wanted, near_blocks, tiles):
    return pl.pallas_call(
        sparse_kernel,
        out_shape=jax.ShapeDtypeStruct((TILE, NB * F), jnp.float32),
        in_specs=[SMEM] * 4 + [VMEM] * 5,
        out_specs=VMEM,
        scratch_shapes=[pltpu.VMEM((2 * SOURCES + 1, TILE, NB * F), jnp.bfloat16)],
        cost_estimate=pl.CostEstimate(flops=2 * KS * TILE**3, bytes_accessed=2 * KS * TILE**2, transcendentals=0),
        compiler_params=pltpu.CompilerParams(vmem_limit_bytes=16 << 20),
        name="sparse_sums",
    )(row, src, count, wanted, *near_blocks, tiles)


def collect_kernel(own_ref, other_ref, out_ref, sems):
    core = lax.axis_index("blk") % NC
    copies = [
        pltpu.make_async_copy(tiles_ref.at[z, :, :, core], out_ref.at[side, z], sems.at[side, z])
        for side, tiles_ref in enumerate((own_ref, other_ref))
        for z in range(NZ)
    ]
    for copy in copies:
        copy.start()
    for copy in copies:
        copy.wait()


def collect(own, other):
    shape = (NZ, NX, NY, NC, TILE, TILE)
    return pl.pallas_call(
        collect_kernel,
        out_shape=jax.ShapeDtypeStruct((NC, NZ, NX, NY, TILE, TILE), jnp.bfloat16),
        in_specs=[HBM, HBM],
        out_specs=VMEM,
        scratch_shapes=[pltpu.SemaphoreType.DMA((NC, NZ))],
        compiler_params=pltpu.CompilerParams(vmem_limit_bytes=44 << 20),
        cost_estimate=pl.CostEstimate(flops=0, bytes_accessed=2 * SHARDS * TILE**2, transcendentals=0),
        name="collect",
    )(own.reshape(shape), other.reshape(shape))


def dense_kernel(halves, turns, shift, own_row_ref, other_row_ref, *refs):
    chunk_refs, (tiles_ref, start_ref, out_ref) = refs[:halves], refs[halves:]
    me = lax.axis_index("blk")
    x, y, core = me // (NY * NC) % NX, me // NC % NY, me % NC
    fixed = (jnp.where(core == 0, x, y) + shift) % SIDE
    out_ref[...] = start_ref[...]
    for k, turn in enumerate(turns):
        chunk_ref, at = chunk_refs[k * halves // len(turns)], k % (len(turns) // halves)
        along = (jnp.where(core == 0, y, x) + turn) % SIDE
        at_x = jnp.where(core == 0, fixed, along)
        at_y = jnp.where(core == 0, along, fixed)
        sources = [((z * NX + at_x) * NY + at_y) * NC + core for z in range(NZ)]
        for side, row_ref in enumerate((own_row_ref, other_row_ref)):
            left = jnp.concatenate([tiles_ref[side, z, at_x, at_y] for z in range(NZ)], axis=1)
            right = jnp.concatenate(
                [placed_pair(chunk_ref[at, z], row_ref[source]) for z, source in enumerate(sources)], axis=0
            )
            out_ref[side] += jnp.dot(left, right, preferred_element_type=jnp.float32)


def dense_part(shift, rows, chunks, tiles, start, turns=TURNS):
    return pl.pallas_call(
        functools.partial(dense_kernel, len(chunks), turns, shift),
        out_shape=jax.ShapeDtypeStruct((NC, TILE, NB * F), jnp.float32),
        in_specs=[SMEM] * 2 + [VMEM] * (len(chunks) + 2),
        out_specs=VMEM,
        compiler_params=pltpu.CompilerParams(vmem_limit_bytes=16 << 20),
        cost_estimate=pl.CostEstimate(
            flops=4 * NC * len(turns) * NZ * TILE**3,
            bytes_accessed=6 * len(turns) * NZ * TILE**2,
            transcendentals=0,
        ),
        name="dense_part",
    )(*rows, *chunks, tiles, start)


def finish_kernel(wide, hub_ref, dense_ref, other_ref, sparse_ref, weight_ref, out_ref, *copies):
    blocks = []
    for block in range(NB):
        columns = slice(block * F, (block + 1) * F)
        summed = dense_ref[0, :, columns] + other_ref[:, columns] + sparse_ref[:, columns]
        projected = jnp.dot(
            summed, weight_ref[...], precision=lax.Precision.HIGHEST, preferred_element_type=jnp.float32
        )
        blocks.append(jnp.maximum(projected, 0.0).astype(out_ref.dtype))
        out_ref[block] = blocks[block]
    if wide:
        hub = jnp.where(hub_ref[lax.axis_index("blk")] == 0, blocks[0], blocks[1])
        for z in range(NZ):
            copies[0][z] = hub


def finish(hub_block, dense, other, sparse, weight, dtype, wide):
    shape = jax.ShapeDtypeStruct((NB, TILE, F), dtype)
    copies = [jax.ShapeDtypeStruct((NZ, TILE, F), dtype)] if wide else []
    return pl.pallas_call(
        functools.partial(finish_kernel, wide),
        out_shape=(shape, *copies),
        in_specs=[SMEM] + [VMEM] * 4,
        out_specs=(VMEM,) * (1 + len(copies)),
        compiler_params=pltpu.CompilerParams(vmem_limit_bytes=8 << 20),
        name="finish",
    )(hub_block, dense, other, sparse, weight)


def shards(
    features,
    weight_one,
    weight_two,
    dense_tiles,
    dense_row,
    hub_block,
    sparse_tiles,
    sparse_row,
    sparse_src,
    sparse_count,
    fetch_list,
):
    rows = [dense_row, swap_cores(dense_row)]
    other_tiles = swap_cores(dense_tiles)
    zeros = jnp.zeros((NC, TILE, NB * F), jnp.float32)

    def propagate(blocks, copies, weight, dtype, wide, tiles=None):
        column = lax.all_to_all(copies, "blk", 0, 0, axis_index_groups=groups_along_z(), tiled=True)
        blocks, column = lax.optimization_barrier((blocks, column))
        beside = swap_cores(blocks)
        pair = jnp.stack([blocks, beside])
        side_behind = step(column, 1, True)
        side_ahead = step(column, -1, True)
        opposite = step(column, 2, True)
        fetched = from_chips(pair)
        first = jnp.stack([column, side_behind])
        last = jnp.stack([side_ahead, opposite])
        if tiles is None:
            tiles = collect(dense_tiles, lax.optimization_barrier((first, other_tiles))[1])
        behind_first = step(first, 1, False)
        ahead_last = step(last, -1, False)
        behind_last, ahead_first = step(last, 1, False), step(first, -1, False)
        shared = swap_cores(fetched)
        far = (step(behind_first, 1, False), step(ahead_last, -1, False))
        total = dense_part(0, rows, (first, last), tiles, zeros)
        near_blocks, total = lax.optimization_barrier(((blocks, beside, fetched, shared), total))
        sparse = sparse_sums(sparse_row, sparse_src, sparse_count, fetch_list, near_blocks, sparse_tiles)
        total = dense_part(SIDE - 1, rows, (behind_first, behind_last), tiles, total)
        total = dense_part(1, rows, (ahead_first, ahead_last), tiles, total)
        far_first, total, sparse = lax.optimization_barrier((far[0], total, sparse))
        total = dense_part(2, rows, (far_first,), tiles, total, TURNS[: SIDE // 2])
        total = dense_part(2, rows, (far[1],), tiles, total, TURNS[SIDE // 2 :])
        returned = swap_cores(total[1])
        return *finish(hub_block, total, returned, sparse, weight, dtype, wide), tiles

    blocks, copies = enter(hub_block, features)
    hidden, copies, tiles = propagate(blocks, copies, weight_one, jnp.bfloat16, True)
    embedded, _ = propagate(hidden, copies, weight_two, jnp.float32, False, tiles)
    return embedded.reshape(NB * TILE, F)


def solution(mesh):
    placed = (
        P("blk", None),
        P(),
        P(),
        P("blk", None, None),
        P("blk"),
        P(),
        P("blk", None, None),
        P("blk"),
        P("blk"),
        P("blk"),
        P("blk", None),
    )
    return jax.shard_map(shards, mesh=mesh, in_specs=placed, out_specs=P("blk", None), check_vma=False)
```
